32 devices in a mesh: vocab: 8 (over z, x), batch: 4 (over y, core).
Axes of the slice: x: 2, y: 2, z: 4, core: 2. Of those that a mesh axis runs over, the one named last changes fastest.
Arguments:
- hidden: bfloat16 [256, 1024], P(('vocab', 'batch'))
- embedding: bfloat16 [8192, 1024], P('vocab')
- block_counts: int32 [64], P('vocab'), may hold values from 1 to 4095
- lang_blocks: int32 [200, 64], replicated, may hold values from -1 to 63, as said below
- sent_lang: int32 [4], replicated, may hold values from 0 to 199
- targets: int32 [256], replicated, may hold values from 0 to 8191, as said below
Outputs:
- token_loss: float32 [256], P(('vocab', 'batch'))
- grad_embed: bfloat16 [8192, 1024], P(('vocab', 'batch'))
The draws below stay inside these ranges and needn't reach their ends.
Inputs may be any that keep to these rules, and one draw needn't show every extreme that they name: `lang_blocks`: each list holds distinct block numbers and then -1 padding; the first entry of every list is block 0; at least 16 entries are blocks, and some language fills all 64 entries. `targets`: the target of token t lies in a block listed for the language of sentence t // 64.
All inputs are finite; a program needn't handle non-finite values.
Results may differ from the reference program's by a relative error of at most 0.0075.
Values may be sent and summed in bfloat16 or wider, within the bound.
No kernel may reach another device: no remote copies, remote signals or barrier semaphores. Data moves between devices by JAX's collectives and lax.ppermute only.
A program may use at most 64 MiB of HBM per device.

```python
import math
import jax
import jax.numpy as jnp
from jax import lax

D = 1024
BLOCK = 128
LANGS = 200
LB = 64
SEQ = 64
TOK_DEV = 8
NBLK = 64
VOCAB = 8192
TOKENS = 256
SENTS = 4
N_BATCH = 4


def first_block(key):
    spread = 3.0 / math.sqrt(D)
    return jax.random.truncated_normal(jax.random.fold_in(key, 401), -6.0, 6.0, (BLOCK, D), jnp.float32) * spread


def language_lists(key):
    base_key = jax.random.fold_in(key, 101)

    def one_language(language):
        shuffled = jax.random.permutation(jax.random.fold_in(base_key, language), NBLK - 1) + 1
        return shuffled[:LB - 1].astype(jnp.int32)
    chosen = jax.vmap(one_language)(jnp.arange(LANGS, dtype=jnp.int32))
    lists = jnp.concatenate([jnp.zeros((LANGS, 1), jnp.int32), chosen], axis=1)
    full_language = LANGS - 1
    full_rest = (jax.random.permutation(jax.random.fold_in(key, 105), NBLK - 2) + 1)[:LB - 2].astype(jnp.int32)
    full_row = jnp.concatenate([jnp.zeros((1,), jnp.int32), jnp.full((1,), NBLK - 1, jnp.int32), full_rest])
    lists = lists.at[full_language].set(full_row)
    counts = jax.random.randint(jax.random.fold_in(key, 102), (LANGS,), LB // 4, LB + 1)
    short_language = jax.random.randint(jax.random.fold_in(key, 104), (), 0, LANGS - 1)
    language_ids = jnp.arange(LANGS, dtype=jnp.int32)
    counts = jnp.where(language_ids == full_language, LB, counts)
    counts = jnp.where(language_ids == short_language, LB // 4, counts)
    padded = jnp.where(jnp.arange(LB, dtype=jnp.int32)[None, :] < counts[:, None], lists, -1)
    return (padded.astype(jnp.int32), counts.astype(jnp.int32))


def sentence_languages(key):
    drawn = jax.random.randint(jax.random.fold_in(key, 201), (SENTS,), 0, LANGS).astype(jnp.int32)
    drawn = drawn.at[0].set(0)
    return drawn.at[SENTS - 1].set(LANGS - 1).astype(jnp.int32)


def draw_lang_blocks(key, part):
    return language_lists(key)[0]


def draw_sent_lang(key, part):
    return sentence_languages(key)


def draw_targets(key, part):
    lists, counts = language_lists(key)
    languages = sentence_languages(key)
    token_language = jnp.repeat(languages, SEQ)
    position = jax.random.randint(jax.random.fold_in(key, 301), (TOKENS,), 0, LB) % counts[token_language]
    chosen_block = lists[token_language, position]
    within = jax.random.randint(jax.random.fold_in(key, 302), (TOKENS,), 0, BLOCK)
    drawn = (chosen_block * BLOCK + within).astype(jnp.int32)
    drawn = drawn.at[0].set(0)
    return drawn.at[TOKENS - 1].set(VOCAB - 1).astype(jnp.int32)


def draw_embedding(key, part):
    spread = 3.0 / math.sqrt(D)
    remainder = jax.random.truncated_normal(jax.random.fold_in(key, 402), -6.0, 6.0, (VOCAB - BLOCK, D), jnp.float32) * spread
    return jnp.concatenate([first_block(key), remainder], axis=0).astype(jnp.bfloat16)


def draw_hidden(key, part):
    return jax.random.truncated_normal(jax.random.fold_in(key, 502), -6.0, 6.0, (TOKENS, D), jnp.float32).astype(jnp.bfloat16)


def with_ends(values, rng, least, top_value):
    longest = values.shape.index(max(values.shape))
    spots = []
    for shift in (0, 1):
        where = [jax.random.randint(jax.random.fold_in(rng, axis), (), 0, length) for axis, length in enumerate(values.shape)]
        where[longest] = (where[longest] + shift) % values.shape[longest]
        spots.append(tuple(where))
    return values.at[spots[0]].set(least).at[spots[1]].set(top_value)


def setup_inputs(seed: int = 0) -> dict:
    seeds = jax.random.split(jax.random.key(seed), 7)
    return {
        "hidden": draw_hidden(jax.random.fold_in(seeds[6], 71), 0),
        "embedding": draw_embedding(jax.random.fold_in(seeds[6], 71), 0),
        "block_counts": with_ends(jax.random.randint(seeds[2], (NBLK,), 1, 4096), jax.random.fold_in(seeds[2], 1), 1, 4095).astype(jnp.int32),
        "lang_blocks": draw_lang_blocks(jax.random.fold_in(seeds[6], 71), 0),
        "sent_lang": draw_sent_lang(jax.random.fold_in(seeds[6], 71), 0),
        "targets": draw_targets(jax.random.fold_in(seeds[6], 71), 0),
    }


def sentence_terms(hidden, embedding, log_sampling, lang_blocks, sent_lang, targets, sentence_index):
    blocks = lang_blocks[sent_lang[sentence_index]]
    usable = blocks >= 0
    safe_blocks = jnp.where(usable, blocks, 0).astype(jnp.int32)
    row_ids = (safe_blocks[:, None] * BLOCK + jnp.arange(BLOCK, dtype=jnp.int32)[None, :]).reshape(-1)
    candidates = jnp.take(embedding, row_ids, axis=0)
    first_token = (sentence_index * SEQ).astype(jnp.int32)
    hidden_rows = lax.dynamic_slice_in_dim(hidden, first_token, SEQ, 0)
    target_ids = lax.dynamic_slice_in_dim(targets, first_token, SEQ, 0)
    raw_scores = lax.dot_general(hidden_rows, candidates, (((1,), (1,)), ((), ())), preferred_element_type=jnp.float32)
    logits = raw_scores.reshape(SEQ, LB, BLOCK) - log_sampling[safe_blocks][None, :, None]
    allowed = usable[None, :, None]
    peak_value = jnp.max(jnp.where(allowed, logits, -jnp.inf), axis=(1, 2))
    denominator = jnp.sum(jnp.where(allowed, jnp.exp(logits - peak_value[:, None, None]), 0.0), axis=(1, 2))
    log_total = peak_value + jnp.log(denominator)
    is_target = (row_ids.reshape(LB, BLOCK)[None, :, :] == target_ids[:, None, None]) & allowed
    target_logit = jnp.sum(jnp.where(is_target, logits, 0.0), axis=(1, 2))
    loss_part = log_total - target_logit
    softmax_weights = jnp.where(allowed, jnp.exp(logits - log_total[:, None, None]), 0.0)
    grad_logits = (softmax_weights - is_target.astype(jnp.float32)).astype(jnp.bfloat16).reshape(SEQ, LB * BLOCK)
    token_group = ((jnp.arange(SEQ, dtype=jnp.int32) + first_token) // TOK_DEV) % N_BATCH
    return loss_part, grad_logits, row_ids, usable, hidden_rows, token_group


def reference(hidden, embedding, block_counts, lang_blocks, sent_lang, targets):
    log_sampling = jnp.log(block_counts.astype(jnp.float32))
    sentence_list = jnp.arange(SENTS, dtype=jnp.int32)

    def loss_only(sentence_index):
        return sentence_terms(hidden, embedding, log_sampling, lang_blocks, sent_lang, targets, sentence_index)[0]

    token_loss = lax.map(loss_only, sentence_list).reshape(-1)
    summed = jnp.zeros((VOCAB, D), jnp.float32)
    for source in range(N_BATCH):
        def add_sentence(accumulated, sentence_index):
            loss_part, grad_logits, row_ids, usable, hidden_rows, token_group = sentence_terms(
                hidden, embedding, log_sampling, lang_blocks, sent_lang, targets, sentence_index)
            keep = token_group == source
            weighted = jnp.where(keep[:, None], grad_logits, jnp.zeros_like(grad_logits))
            contribution = lax.dot_general(weighted, hidden_rows, (((0,), (0,)), ((), ())), preferred_element_type=jnp.float32)
            contribution = contribution * jnp.repeat(usable, BLOCK)[:, None].astype(jnp.float32)
            return accumulated.at[row_ids].add(contribution), None

        accumulated, ignored = lax.scan(add_sentence, jnp.zeros((VOCAB, D), jnp.float32), sentence_list)
        rounded = lax.optimization_barrier(accumulated.astype(jnp.bfloat16))
        summed = summed + rounded.astype(jnp.float32)
    return token_loss, summed.astype(jnp.bfloat16)
```

```python
import jax
import jax.numpy as jnp
from jax import lax
from jax.sharding import PartitionSpec as P

SEQ = 64


masked_fill = float(jnp.finfo(jnp.float32).min)


def centre_first(count):
    return sorted(range(count), key=lambda i: (abs(i // 2 - count // 4), i // 2, -i))


def body(hidden, embedding, block_counts, lang_blocks, sent_lang, targets):
    tok_dev, width = hidden.shape
    vocab_count = lax.axis_size("vocab")
    batch_count = lax.axis_size("batch")
    vocab_index = lax.axis_index("vocab")
    batch_index = lax.axis_index("batch")
    local_rows = embedding.shape[0]
    local_blocks = block_counts.shape[0]
    block_width = local_rows // local_blocks
    own_rows = local_rows // batch_count
    own_blocks = own_rows // block_width
    group_tokens = vocab_count * tok_dev
    order = centre_first(vocab_count)
    both = ("vocab", "batch")
    groups = [[v * batch_count + b for v in order] for b in range(batch_count)]

    copies = jnp.broadcast_to(hidden[None], (vocab_count, tok_dev, width))
    gathered = lax.all_to_all(copies, both, 0, 0, tiled=True, axis_index_groups=groups)
    gathered = gathered.reshape(group_tokens, width)
    pieces = [gathered]
    for step in range(1, batch_count):
        pairs = [(b, b ^ step) for b in range(batch_count)]
        pieces.append(lax.ppermute(gathered, "batch", pairs))
    everyone = jnp.concatenate(pieces, axis=0)

    sources = batch_index ^ jnp.arange(batch_count, dtype=jnp.int32)
    places = jnp.array(order, jnp.int32)
    token_ids = (
        (places[None, :, None] * batch_count + sources[:, None, None]) * tok_dev
        + jnp.arange(tok_dev, dtype=jnp.int32)[None, None, :]
    ).reshape(batch_count, group_tokens)
    target_table = targets.reshape(vocab_count, batch_count, tok_dev)
    target_table = jnp.stack([target_table[v] for v in order], axis=1)
    target_ids = jnp.stack(
        [
            lax.dynamic_index_in_dim(target_table, batch_index ^ step, 0, keepdims=False)
            for step in range(batch_count)
        ]
    ).reshape(batch_count, group_tokens)

    block_ids = vocab_index * local_blocks + jnp.arange(local_blocks, dtype=jnp.int32)
    sentence_lists = lang_blocks[sent_lang]
    member = jnp.any(sentence_lists[:, None, :] == block_ids[None, :, None], axis=2)
    sentence_ids = jnp.arange(sent_lang.shape[0], dtype=jnp.int32)
    sentence_hit = (token_ids // SEQ)[None] == sentence_ids[:, None, None]
    allowed = jnp.any(member[:, :, None, None] & sentence_hit[:, None], axis=0)
    log_sampling = jnp.log(block_counts.astype(jnp.float32))

    own_allowed = allowed[:, 0][:, None, :]
    logits = lax.dot_general(
        embedding, gathered, (((1,), (1,)), ((), ())), preferred_element_type=jnp.float32
    ).reshape(local_blocks, block_width, group_tokens) - log_sampling[:, None, None]
    word_ids = (vocab_index * local_rows + jnp.arange(local_rows, dtype=jnp.int32)).reshape(
        local_blocks, block_width
    )
    is_target = word_ids[:, :, None] == target_ids[0][None, None, :]
    local_peak = jnp.max(jnp.where(own_allowed, logits, masked_fill), axis=(0, 1))
    local_total = jnp.sum(
        jnp.where(own_allowed, jnp.exp(logits - local_peak[None, None, :]), 0.0), axis=(0, 1)
    )
    local_target = jnp.sum(jnp.where(is_target, logits, 0.0), axis=(0, 1))
    blank = jnp.zeros_like(local_peak)
    stats = jnp.stack([local_peak, local_total, local_target] + [blank] * 5)
    stats = jnp.broadcast_to(stats[None], (vocab_count * batch_count,) + stats.shape)
    stats = lax.all_to_all(stats, both, 0, 0, tiled=True)
    stats = stats.reshape(vocab_count, batch_count, 8, group_tokens)
    peak = jnp.max(stats[:, :, 0], axis=0)
    total = jnp.sum(stats[:, :, 1] * jnp.exp(stats[:, :, 0] - peak[None]), axis=0)
    log_total = peak + jnp.log(total)
    target_logit = jnp.sum(stats[:, :, 2], axis=0)
    every_loss = lax.dynamic_index_in_dim(log_total - target_logit, batch_index, 0, keepdims=False)
    my_place = jnp.sum(jnp.where(places == vocab_index, jnp.arange(vocab_count), 0))
    token_loss = lax.dynamic_slice_in_dim(every_loss, my_place * tok_dev, tok_dev, 0)
    ordered = jnp.stack(
        [
            lax.dynamic_index_in_dim(log_total, batch_index ^ step, 0, keepdims=False)
            for step in range(batch_count)
        ]
    ).reshape(-1)

    mine = lax.dynamic_slice_in_dim(embedding, batch_index * own_rows, own_rows, 0)
    my_blocks = batch_index * own_blocks
    my_sampling = lax.dynamic_slice_in_dim(log_sampling, my_blocks, own_blocks, 0)
    my_allowed = lax.dynamic_slice_in_dim(allowed, my_blocks, own_blocks, 0)
    my_allowed = my_allowed.reshape(own_blocks, 1, -1)
    my_words = lax.dynamic_slice_in_dim(word_ids, my_blocks, own_blocks, 0)
    my_logits = lax.dot_general(
        mine, everyone, (((1,), (1,)), ((), ())), preferred_element_type=jnp.float32
    ).reshape(own_blocks, block_width, -1) - my_sampling[:, None, None]
    weights = jnp.where(my_allowed, jnp.exp(my_logits - ordered[None, None, :]), 0.0)
    hits = my_words[:, :, None] == target_ids.reshape(-1)[None, None, :]
    grad_logits = (weights - hits.astype(jnp.float32)).astype(jnp.bfloat16)
    grad_embed = lax.dot_general(
        grad_logits.reshape(own_rows, -1),
        everyone,
        (((1,), (0,)), ((), ())),
        preferred_element_type=jnp.float32,
    ).astype(jnp.bfloat16)
    return (token_loss, grad_embed)


def solution(mesh):
    in_specs = (P(("vocab", "batch"), None), P("vocab", None), P("vocab"), P(), P(), P())
    out_specs = (P(("vocab", "batch")), P(("vocab", "batch"), None))
    return jax.shard_map(body, mesh=mesh, in_specs=in_specs, out_specs=out_specs, check_vma=False)
```

```python
import functools

import jax
import jax.numpy as jnp
from jax import lax
from jax.experimental import pallas as pl
from jax.experimental.pallas import tpu as pltpu
from jax.sharding import PartitionSpec as P

SEQ = 64
LANES = 128
KERNEL_VMEM = 8 * 1024 * 1024


masked_fill = float(jnp.finfo(jnp.float32).min)


def centre_first(count):
    return sorted(range(count), key=lambda i: (abs(i // 2 - count // 4), i // 2, -i))


def iota(shape, axis):
    return lax.broadcasted_iota(jnp.int32, shape, axis)


def contract_last(a, b):
    return lax.dot_general(a, b, (((1,), (1,)), ((), ())), preferred_element_type=jnp.float32)


def prepare_kernel(
    order, tok_dev, batch_count, sent_hbm, count_hbm, lists_hbm, targets_hbm, emb_hbm,
    bias_ref, target_ref, kept_ref, sent_ref, count_ref, lists_ref, targets_ref, sems,
):
    sources = (sent_hbm, count_hbm, lists_hbm, targets_hbm, emb_hbm)
    places = (sent_ref, count_ref, lists_ref, targets_ref, kept_ref)
    fetches = [
        pltpu.make_async_copy(src, dst, sems.at[i])
        for i, (src, dst) in enumerate(zip(sources, places))
    ]
    for fetch in fetches:
        fetch.start()
    vocab_index = lax.axis_index("vocab")
    batch_index = lax.axis_index("batch")
    local_blocks, tokens = bias_ref.shape
    group_tokens = tokens // batch_count
    languages = lists_ref.shape[1]

    lane = iota((1, tokens), 1)
    source = batch_index ^ (lane // group_tokens)
    position = (lane % group_tokens) // tok_dev
    place = jnp.zeros((1, tokens), jnp.int32)
    for j, v in enumerate(order):
        place = jnp.where(position == j, v, place)
    token = (place * batch_count + source) * tok_dev + lane % tok_dev
    sentence = token // SEQ

    for fetch in fetches[:-1]:
        fetch.wait()
    found = jnp.zeros((1, tokens), jnp.float32)
    for start in range(0, tokens, LANES):
        size = min(LANES, tokens - start)
        part = targets_ref[:, start : start + size].astype(jnp.float32)
        eye = iota((size, size), 0) == iota((size, size), 1)
        column = jnp.sum(jnp.where(eye, part, 0.0), axis=1, keepdims=True)
        hit = (iota((size, tokens), 0) + start) == token
        found = found + jnp.sum(jnp.where(hit, column, 0.0), axis=0, keepdims=True)
    target_ref[...] = found.astype(jnp.int32)

    block = iota((local_blocks, 1), 0)
    member = jnp.zeros((local_blocks, languages), jnp.float32)
    counts = jnp.zeros((local_blocks, 1), jnp.float32)
    for k in range(local_blocks):
        listed = jnp.where(lists_ref[...] == vocab_index * local_blocks + k, 1.0, 0.0)
        listed = jnp.max(listed, axis=0, keepdims=True)
        member = jnp.where(block == k, listed, member)
        counts = jnp.where(block == k, count_ref[k].astype(jnp.float32), counts)
    log_counts = jnp.log(counts)
    bias = jnp.full((local_blocks, tokens), jnp.inf, jnp.float32)
    language = iota((local_blocks, languages), 1)
    for s in range(sent_ref.shape[0]):
        picked = jnp.where(language == sent_ref[s], member, 0.0)
        picked = jnp.max(picked, axis=1, keepdims=True)
        bias = jnp.where((sentence == s) & (picked > 0.5), log_counts, bias)
    bias_ref[...] = bias
    fetches[-1].wait()


def stats_kernel(bias_ref, target_ref, emb_ref, rows_ref, stats_ref, logits_ref):
    vocab_index = lax.axis_index("vocab")
    group_tokens = rows_ref.shape[0]
    local_rows = emb_ref.shape[0]
    local_blocks = bias_ref.shape[0]
    block_width = local_rows // local_blocks

    raw = contract_last(emb_ref[...], rows_ref[...])
    own_target = target_ref[:, :group_tokens] - vocab_index * local_rows
    top = jnp.full((block_width, group_tokens), -jnp.inf, jnp.float32)
    aimed = jnp.zeros((block_width, group_tokens), jnp.float32)
    for k in range(local_blocks):
        rows = slice(k * block_width, (k + 1) * block_width)
        cell = bias_ref[k : k + 1, :group_tokens]
        logits = jnp.where(cell < jnp.inf, raw[rows] - cell, -jnp.inf)
        logits_ref[rows, :] = logits
        top = jnp.maximum(top, logits)
        word = iota((block_width, group_tokens), 0) + k * block_width
        aimed = jnp.where(word == own_target, logits, aimed)
    peak = jnp.maximum(jnp.max(top, axis=0, keepdims=True), masked_fill)
    total = jnp.zeros((block_width, group_tokens), jnp.float32)
    for k in range(local_blocks):
        rows = slice(k * block_width, (k + 1) * block_width)
        total = total + jnp.exp(logits_ref[rows, :] - peak)
    total = jnp.sum(total, axis=0, keepdims=True)
    aimed = jnp.sum(aimed, axis=0, keepdims=True)
    row = iota((8, group_tokens), 0)
    packed = jnp.where(row == 0, peak, jnp.where(row == 1, total, aimed))
    for p in range(stats_ref.shape[0]):
        for start in range(0, LANES, group_tokens):
            stats_ref[p, :, start : start + group_tokens] = packed


def grad_kernel(
    order, tok_dev, batch_count, stats_ref, bias_ref, target_ref, emb_ref, *refs
):
    row_refs = refs[:batch_count]
    loss_ref, grad_ref, weight_ref, everyone_ref = refs[batch_count:]
    vocab_index = lax.axis_index("vocab")
    batch_index = lax.axis_index("batch")
    group_tokens = row_refs[0].shape[0]
    own_rows = grad_ref.shape[0]
    local_blocks = bias_ref.shape[0]
    local_rows = emb_ref.shape[0]
    block_width = local_rows // local_blocks
    own_blocks = own_rows // block_width
    vocab_count = stats_ref.shape[0] // batch_count

    for m in range(batch_count):
        everyone_ref[m * group_tokens : (m + 1) * group_tokens, :] = row_refs[m][...]
    mine = emb_ref[pl.ds(pl.multiple_of(batch_index * own_rows, own_rows), own_rows), :]
    raw = contract_last(mine, everyone_ref[...])
    biases = [bias_ref[pl.ds(batch_index * own_blocks + k, 1), :] for k in range(own_blocks)]

    for m in range(batch_count):
        group = batch_index ^ m
        parts = [stats_ref[v * batch_count + group] for v in range(vocab_count)]
        peak = parts[0][0:1]
        for part in parts[1:]:
            peak = jnp.maximum(peak, part[0:1])
        total = jnp.zeros_like(peak)
        for part in parts:
            total = total + part[1:2] * jnp.exp(part[0:1] - peak)
        log_total = (peak + jnp.log(total))[:, :group_tokens]
        if m == 0:
            aimed = jnp.zeros_like(peak)
            for part in parts:
                aimed = aimed + part[2:3]
            loss = log_total - aimed[:, :group_tokens]
            my_place = jnp.int32(0)
            for j, v in enumerate(order):
                my_place = jnp.where(vocab_index == v, j, my_place)
            wanted = my_place * tok_dev + iota((tok_dev, group_tokens), 0)
            chosen = jnp.where(iota((tok_dev, group_tokens), 1) == wanted, loss, 0.0)
            chosen = jnp.sum(chosen, axis=1, keepdims=True)
            eye = iota((tok_dev, tok_dev), 0) == iota((tok_dev, tok_dev), 1)
            loss_ref[...] = jnp.sum(jnp.where(eye, chosen, 0.0), axis=0, keepdims=True)
        lanes = slice(m * group_tokens, (m + 1) * group_tokens)
        target = target_ref[:, lanes] - vocab_index * local_rows - batch_index * own_rows
        for k in range(own_blocks):
            rows = slice(k * block_width, (k + 1) * block_width)
            cell = biases[k][:, lanes]
            logits = raw[rows, lanes] - cell
            weight = jnp.where(cell < jnp.inf, jnp.exp(logits - log_total), 0.0)
            word = iota((block_width, group_tokens), 0) + k * block_width
            weight = weight - jnp.where(word == target, 1.0, 0.0)
            weight_ref[rows, lanes] = weight.astype(jnp.bfloat16)
    grad_ref[...] = jnp.dot(
        weight_ref[...], everyone_ref[...], preferred_element_type=jnp.float32
    ).astype(grad_ref.dtype)


VMEM = pl.BlockSpec(memory_space=pltpu.VMEM)


def fused_body(hidden, embedding, block_counts, lang_blocks, sent_lang, targets):
    tok_dev, width = hidden.shape
    vocab_count = lax.axis_size("vocab")
    batch_count = lax.axis_size("batch")
    local_rows = embedding.shape[0]
    local_blocks = block_counts.shape[0]
    own_rows = local_rows // batch_count
    group_tokens = vocab_count * tok_dev
    tokens = group_tokens * batch_count
    devices = vocab_count * batch_count
    order = centre_first(vocab_count)
    both = ("vocab", "batch")
    groups = [[v * batch_count + b for v in order] for b in range(batch_count)]
    struct = jax.ShapeDtypeStruct

    copies = jnp.broadcast_to(hidden[None], (vocab_count, tok_dev, width))
    gathered = lax.all_to_all(copies, both, 0, 0, tiled=True, axis_index_groups=groups)
    gathered = gathered.reshape(group_tokens, width)
    pieces = [gathered]
    for step in range(1, batch_count):
        pairs = [(b, b ^ step) for b in range(batch_count)]
        pieces.append(lax.ppermute(gathered, "batch", pairs))

    limit = pltpu.CompilerParams(vmem_limit_bytes=KERNEL_VMEM)
    bias, target_ids, kept = pl.pallas_call(
        functools.partial(prepare_kernel, order, tok_dev, batch_count),
        out_shape=(
            struct((local_blocks, tokens), jnp.float32),
            struct((1, tokens), jnp.int32),
            struct(embedding.shape, embedding.dtype),
        ),
        in_specs=[pl.BlockSpec(memory_space=pltpu.HBM)] * 5,
        out_specs=(VMEM, VMEM, VMEM),
        scratch_shapes=[
            pltpu.SMEM(sent_lang.shape, jnp.int32),
            pltpu.SMEM(block_counts.shape, jnp.int32),
            pltpu.VMEM(lang_blocks.shape[::-1], jnp.int32),
            pltpu.VMEM((1, tokens), jnp.int32),
            pltpu.SemaphoreType.DMA((5,)),
        ],
        compiler_params=limit,
        name="prepare",
        cost_estimate=pl.CostEstimate(
            flops=tokens * tokens, bytes_accessed=4 * local_rows * width, transcendentals=0
        ),
    )(
        *(
            pltpu.with_memory_space_constraint(x, pltpu.HBM)
            for x in (sent_lang, block_counts, lang_blocks.T, targets.reshape(1, -1), embedding)
        )
    )
    stats = pl.pallas_call(
        stats_kernel,
        out_shape=struct((devices, 8, LANES), jnp.float32),
        in_specs=[VMEM] * 4,
        out_specs=VMEM,
        scratch_shapes=[pltpu.VMEM((local_rows, group_tokens), jnp.float32)],
        compiler_params=limit,
        name="stats",
        cost_estimate=pl.CostEstimate(
            flops=2 * local_rows * group_tokens * width,
            bytes_accessed=2 * local_rows * width,
            transcendentals=local_rows * group_tokens,
        ),
    )(bias, target_ids, kept, gathered)
    stats = lax.all_to_all(stats, both, 0, 0, tiled=True)
    loss, grad = pl.pallas_call(
        functools.partial(grad_kernel, order, tok_dev, batch_count),
        out_shape=(struct((1, tok_dev), jnp.float32), struct((own_rows, width), jnp.bfloat16)),
        in_specs=[VMEM] * (4 + batch_count),
        out_specs=(VMEM, VMEM),
        scratch_shapes=[
            pltpu.VMEM((own_rows, tokens), jnp.bfloat16),
            pltpu.VMEM((tokens, width), jnp.bfloat16),
        ],
        name="grad",
        compiler_params=limit,
        cost_estimate=pl.CostEstimate(
            flops=4 * own_rows * tokens * width,
            bytes_accessed=2 * own_rows * width,
            transcendentals=own_rows * tokens,
        ),
    )(stats, bias, target_ids, kept, *pieces)
    return (loss.reshape(tok_dev), grad)


def body(hidden, embedding, block_counts, lang_blocks, sent_lang, targets):
    tok_dev, width = hidden.shape
    vocab_count = lax.axis_size("vocab")
    batch_count = lax.axis_size("batch")
    vocab_index = lax.axis_index("vocab")
    batch_index = lax.axis_index("batch")
    local_rows = embedding.shape[0]
    local_blocks = block_counts.shape[0]
    block_width = local_rows // local_blocks
    own_rows = local_rows // batch_count
    own_blocks = own_rows // block_width
    group_tokens = vocab_count * tok_dev
    order = centre_first(vocab_count)
    both = ("vocab", "batch")
    groups = [[v * batch_count + b for v in order] for b in range(batch_count)]

    copies = jnp.broadcast_to(hidden[None], (vocab_count, tok_dev, width))
    gathered = lax.all_to_all(copies, both, 0, 0, tiled=True, axis_index_groups=groups)
    gathered = gathered.reshape(group_tokens, width)
    pieces = [gathered]
    for step in range(1, batch_count):
        pairs = [(b, b ^ step) for b in range(batch_count)]
        pieces.append(lax.ppermute(gathered, "batch", pairs))
    everyone = jnp.concatenate(pieces, axis=0)

    sources = batch_index ^ jnp.arange(batch_count, dtype=jnp.int32)
    places = jnp.array(order, jnp.int32)
    token_ids = (
        (places[None, :, None] * batch_count + sources[:, None, None]) * tok_dev
        + jnp.arange(tok_dev, dtype=jnp.int32)[None, None, :]
    ).reshape(batch_count, group_tokens)
    target_table = targets.reshape(vocab_count, batch_count, tok_dev)
    target_table = jnp.stack([target_table[v] for v in order], axis=1)
    target_ids = jnp.stack(
        [
            lax.dynamic_index_in_dim(target_table, batch_index ^ step, 0, keepdims=False)
            for step in range(batch_count)
        ]
    ).reshape(batch_count, group_tokens)

    block_ids = vocab_index * local_blocks + jnp.arange(local_blocks, dtype=jnp.int32)
    sentence_lists = lang_blocks[sent_lang]
    member = jnp.any(sentence_lists[:, None, :] == block_ids[None, :, None], axis=2)
    sentence_ids = jnp.arange(sent_lang.shape[0], dtype=jnp.int32)
    sentence_hit = (token_ids // SEQ)[None] == sentence_ids[:, None, None]
    allowed = jnp.any(member[:, :, None, None] & sentence_hit[:, None], axis=0)
    log_sampling = jnp.log(block_counts.astype(jnp.float32))

    own_allowed = allowed[:, 0][:, None, :]
    logits = lax.dot_general(
        embedding, gathered, (((1,), (1,)), ((), ())), preferred_element_type=jnp.float32
    ).reshape(local_blocks, block_width, group_tokens) - log_sampling[:, None, None]
    word_ids = (vocab_index * local_rows + jnp.arange(local_rows, dtype=jnp.int32)).reshape(
        local_blocks, block_width
    )
    is_target = word_ids[:, :, None] == target_ids[0][None, None, :]
    local_peak = jnp.max(jnp.where(own_allowed, logits, masked_fill), axis=(0, 1))
    local_total = jnp.sum(
        jnp.where(own_allowed, jnp.exp(logits - local_peak[None, None, :]), 0.0), axis=(0, 1)
    )
    local_target = jnp.sum(jnp.where(is_target, logits, 0.0), axis=(0, 1))
    blank = jnp.zeros_like(local_peak)
    stats = jnp.stack([local_peak, local_total, local_target] + [blank] * 5)
    stats = jnp.broadcast_to(stats[None], (vocab_count * batch_count,) + stats.shape)
    stats = lax.all_to_all(stats, both, 0, 0, tiled=True)
    stats = stats.reshape(vocab_count, batch_count, 8, group_tokens)
    peak = jnp.max(stats[:, :, 0], axis=0)
    total = jnp.sum(stats[:, :, 1] * jnp.exp(stats[:, :, 0] - peak[None]), axis=0)
    log_total = peak + jnp.log(total)
    target_logit = jnp.sum(stats[:, :, 2], axis=0)
    every_loss = lax.dynamic_index_in_dim(log_total - target_logit, batch_index, 0, keepdims=False)
    my_place = jnp.sum(jnp.where(places == vocab_index, jnp.arange(vocab_count), 0))
    token_loss = lax.dynamic_slice_in_dim(every_loss, my_place * tok_dev, tok_dev, 0)
    ordered = jnp.stack(
        [
            lax.dynamic_index_in_dim(log_total, batch_index ^ step, 0, keepdims=False)
            for step in range(batch_count)
        ]
    ).reshape(-1)

    mine = lax.dynamic_slice_in_dim(embedding, batch_index * own_rows, own_rows, 0)
    my_blocks = batch_index * own_blocks
    my_sampling = lax.dynamic_slice_in_dim(log_sampling, my_blocks, own_blocks, 0)
    my_allowed = lax.dynamic_slice_in_dim(allowed, my_blocks, own_blocks, 0)
    my_allowed = my_allowed.reshape(own_blocks, 1, -1)
    my_words = lax.dynamic_slice_in_dim(word_ids, my_blocks, own_blocks, 0)
    my_logits = lax.dot_general(
        mine, everyone, (((1,), (1,)), ((), ())), preferred_element_type=jnp.float32
    ).reshape(own_blocks, block_width, -1) - my_sampling[:, None, None]
    weights = jnp.where(my_allowed, jnp.exp(my_logits - ordered[None, None, :]), 0.0)
    hits = my_words[:, :, None] == target_ids.reshape(-1)[None, None, :]
    grad_logits = (weights - hits.astype(jnp.float32)).astype(jnp.bfloat16)
    grad_embed = lax.dot_general(
        grad_logits.reshape(own_rows, -1),
        everyone,
        (((1,), (0,)), ((), ())),
        preferred_element_type=jnp.float32,
    ).astype(jnp.bfloat16)
    return (token_loss, grad_embed)


def solution(mesh):
    in_specs = (P(("vocab", "batch"), None), P("vocab", None), P("vocab"), P(), P(), P())
    out_specs = (P(("vocab", "batch")), P(("vocab", "batch"), None))

    def step(hidden, *rest):
        group_tokens = hidden.shape[0] * lax.axis_size("vocab")
        chosen = fused_body if LANES % group_tokens == 0 else body
        return chosen(hidden, *rest)

    return jax.shard_map(step, mesh=mesh, in_specs=in_specs, out_specs=out_specs, check_vma=False)
```

```python
import functools

import jax
import jax.numpy as jnp
from jax import lax
from jax.experimental import pallas as pl
from jax.experimental.pallas import tpu as pltpu
from jax.sharding import PartitionSpec as P

SEQ = 64
LANES = 128
KERNEL_VMEM = 8 * 1024 * 1024


masked_fill = float(jnp.finfo(jnp.float32).min)


def centre_first(count):
    return sorted(range(count), key=lambda i: (abs(i // 2 - count // 4), i // 2, -i))


def iota(shape, axis):
    return lax.broadcasted_iota(jnp.int32, shape, axis)


def contract_last(a, b):
    return lax.dot_general(a, b, (((1,), (1,)), ((), ())), preferred_element_type=jnp.float32)


def prepare_kernel(
    order, tok_dev, batch_count, sent_hbm, count_hbm, lists_hbm, targets_hbm, emb_hbm,
    bias_ref, target_ref, kept_ref, sent_ref, count_ref, lists_ref, targets_ref, sems,
):
    sources = (sent_hbm, count_hbm, lists_hbm, targets_hbm, emb_hbm)
    places = (sent_ref, count_ref, lists_ref, targets_ref, kept_ref)
    fetches = [
        pltpu.make_async_copy(src, dst, sems.at[i])
        for i, (src, dst) in enumerate(zip(sources, places))
    ]
    for fetch in fetches:
        fetch.start()
    vocab_index = lax.axis_index("vocab")
    batch_index = lax.axis_index("batch")
    local_blocks, tokens = bias_ref.shape
    group_tokens = tokens // batch_count
    languages = lists_ref.shape[1]

    lane = iota((1, tokens), 1)
    source = batch_index ^ (lane // group_tokens)
    position = (lane % group_tokens) // tok_dev
    place = jnp.zeros((1, tokens), jnp.int32)
    for j, v in enumerate(order):
        place = jnp.where(position == j, v, place)
    token = (place * batch_count + source) * tok_dev + lane % tok_dev
    sentence = token // SEQ

    for fetch in fetches[:-1]:
        fetch.wait()
    found = jnp.zeros((1, tokens), jnp.float32)
    for start in range(0, tokens, LANES):
        size = min(LANES, tokens - start)
        part = targets_ref[:, start : start + size].astype(jnp.float32)
        eye = iota((size, size), 0) == iota((size, size), 1)
        column = jnp.sum(jnp.where(eye, part, 0.0), axis=1, keepdims=True)
        hit = (iota((size, tokens), 0) + start) == token
        found = found + jnp.sum(jnp.where(hit, column, 0.0), axis=0, keepdims=True)
    target_ref[...] = found.astype(jnp.int32)

    block = iota((local_blocks, 1), 0)
    member = jnp.zeros((local_blocks, languages), jnp.float32)
    counts = jnp.zeros((local_blocks, 1), jnp.float32)
    for k in range(local_blocks):
        listed = jnp.where(lists_ref[...] == vocab_index * local_blocks + k, 1.0, 0.0)
        listed = jnp.max(listed, axis=0, keepdims=True)
        member = jnp.where(block == k, listed, member)
        counts = jnp.where(block == k, count_ref[k].astype(jnp.float32), counts)
    log_counts = jnp.log(counts)
    bias = jnp.full((local_blocks, tokens), jnp.inf, jnp.float32)
    language = iota((local_blocks, languages), 1)
    for s in range(sent_ref.shape[0]):
        picked = jnp.where(language == sent_ref[s], member, 0.0)
        picked = jnp.max(picked, axis=1, keepdims=True)
        bias = jnp.where((sentence == s) & (picked > 0.5), log_counts, bias)
    bias_ref[...] = bias
    fetches[-1].wait()


def stats_kernel(bias_ref, target_ref, emb_ref, rows_ref, stats_ref, logits_ref):
    vocab_index = lax.axis_index("vocab")
    group_tokens = rows_ref.shape[0]
    local_rows = emb_ref.shape[0]
    local_blocks = bias_ref.shape[0]
    block_width = local_rows // local_blocks

    raw = contract_last(emb_ref[...], rows_ref[...])
    own_target = target_ref[:, :group_tokens] - vocab_index * local_rows
    top = jnp.full((block_width, group_tokens), -jnp.inf, jnp.float32)
    aimed = jnp.zeros((block_width, group_tokens), jnp.float32)
    for k in range(local_blocks):
        rows = slice(k * block_width, (k + 1) * block_width)
        cell = bias_ref[k : k + 1, :group_tokens]
        logits = jnp.where(cell < jnp.inf, raw[rows] - cell, -jnp.inf)
        logits_ref[rows, :] = logits
        top = jnp.maximum(top, logits)
        word = iota((block_width, group_tokens), 0) + k * block_width
        aimed = jnp.where(word == own_target, logits, aimed)
    peak = jnp.maximum(jnp.max(top, axis=0, keepdims=True), masked_fill)
    total = jnp.zeros((block_width, group_tokens), jnp.float32)
    for k in range(local_blocks):
        rows = slice(k * block_width, (k + 1) * block_width)
        total = total + jnp.exp(logits_ref[rows, :] - peak)
    total = jnp.sum(total, axis=0, keepdims=True)
    aimed = jnp.sum(aimed, axis=0, keepdims=True)
    row = iota((8, group_tokens), 0)
    packed = jnp.where(row == 0, peak, jnp.where(row == 1, total, aimed))
    for p in range(stats_ref.shape[0]):
        for start in range(0, LANES, group_tokens):
            stats_ref[p, :, start : start + group_tokens] = packed


def grad_kernel(
    order, tok_dev, batch_count, stats_ref, bias_ref, target_ref, emb_ref, *refs
):
    row_refs = refs[:batch_count]
    loss_ref, grad_ref, weight_ref, everyone_ref = refs[batch_count:]
    vocab_index = lax.axis_index("vocab")
    batch_index = lax.axis_index("batch")
    group_tokens = row_refs[0].shape[0]
    own_rows = grad_ref.shape[0]
    local_blocks = bias_ref.shape[0]
    local_rows = emb_ref.shape[0]
    block_width = local_rows // local_blocks
    own_blocks = own_rows // block_width
    vocab_count = stats_ref.shape[0] // batch_count

    for m in range(batch_count):
        everyone_ref[m * group_tokens : (m + 1) * group_tokens, :] = row_refs[m][...]
    mine = emb_ref[pl.ds(pl.multiple_of(batch_index * own_rows, own_rows), own_rows), :]
    raw = contract_last(mine, everyone_ref[...])
    biases = [bias_ref[pl.ds(batch_index * own_blocks + k, 1), :] for k in range(own_blocks)]

    for m in range(batch_count):
        group = batch_index ^ m
        parts = [stats_ref[v * batch_count + group] for v in range(vocab_count)]
        peak = parts[0][0:1]
        for part in parts[1:]:
            peak = jnp.maximum(peak, part[0:1])
        total = jnp.zeros_like(peak)
        for part in parts:
            total = total + part[1:2] * jnp.exp(part[0:1] - peak)
        log_total = (peak + jnp.log(total))[:, :group_tokens]
        if m == 0:
            aimed = jnp.zeros_like(peak)
            for part in parts:
                aimed = aimed + part[2:3]
            loss = log_total - aimed[:, :group_tokens]
            my_place = jnp.int32(0)
            for j, v in enumerate(order):
                my_place = jnp.where(vocab_index == v, j, my_place)
            wanted = my_place * tok_dev + iota((tok_dev, group_tokens), 0)
            chosen = jnp.where(iota((tok_dev, group_tokens), 1) == wanted, loss, 0.0)
            chosen = jnp.sum(chosen, axis=1, keepdims=True)
            eye = iota((tok_dev, tok_dev), 0) == iota((tok_dev, tok_dev), 1)
            loss_ref[...] = jnp.sum(jnp.where(eye, chosen, 0.0), axis=0, keepdims=True)
        lanes = slice(m * group_tokens, (m + 1) * group_tokens)
        target = target_ref[:, lanes] - vocab_index * local_rows - batch_index * own_rows
        for k in range(own_blocks):
            rows = slice(k * block_width, (k + 1) * block_width)
            cell = biases[k][:, lanes]
            logits = raw[rows, lanes] - cell
            weight = jnp.where(cell < jnp.inf, jnp.exp(logits - log_total), 0.0)
            word = iota((block_width, group_tokens), 0) + k * block_width
            weight = weight - jnp.where(word == target, 1.0, 0.0)
            weight_ref[rows, lanes] = weight.astype(jnp.bfloat16)
    grad_ref[...] = jnp.dot(
        weight_ref[...], everyone_ref[...], preferred_element_type=jnp.float32
    ).astype(grad_ref.dtype)


VMEM = pl.BlockSpec(memory_space=pltpu.VMEM)


def fused_body(hidden, embedding, block_counts, lang_blocks, sent_lang, targets):
    tok_dev, width = hidden.shape
    vocab_count = lax.axis_size("vocab")
    batch_count = lax.axis_size("batch")
    local_rows = embedding.shape[0]
    local_blocks = block_counts.shape[0]
    own_rows = local_rows // batch_count
    group_tokens = vocab_count * tok_dev
    tokens = group_tokens * batch_count
    devices = vocab_count * batch_count
    order = centre_first(vocab_count)
    both = ("vocab", "batch")
    groups = [[v * batch_count + b for v in order] for b in range(batch_count)]
    struct = jax.ShapeDtypeStruct

    copies = jnp.broadcast_to(hidden[None], (vocab_count, tok_dev, width))
    gathered = lax.all_to_all(copies, both, 0, 0, tiled=True, axis_index_groups=groups)
    gathered = gathered.reshape(group_tokens, width)
    pieces = [gathered]
    step = batch_count // 2
    while step:
        pairs = [(b, b ^ step) for b in range(batch_count)]
        received = [lax.ppermute(piece, "batch", pairs) for piece in pieces]
        pieces = [half for pair in zip(pieces, received) for half in pair]
        step //= 2

    limit = pltpu.CompilerParams(vmem_limit_bytes=KERNEL_VMEM)
    bias, target_ids, kept = pl.pallas_call(
        functools.partial(prepare_kernel, order, tok_dev, batch_count),
        out_shape=(
            struct((local_blocks, tokens), jnp.float32),
            struct((1, tokens), jnp.int32),
            struct(embedding.shape, embedding.dtype),
        ),
        in_specs=[pl.BlockSpec(memory_space=pltpu.HBM)] * 5,
        out_specs=(VMEM, VMEM, VMEM),
        scratch_shapes=[
            pltpu.SMEM(sent_lang.shape, jnp.int32),
            pltpu.SMEM(block_counts.shape, jnp.int32),
            pltpu.VMEM(lang_blocks.shape[::-1], jnp.int32),
            pltpu.VMEM((1, tokens), jnp.int32),
            pltpu.SemaphoreType.DMA((5,)),
        ],
        compiler_params=limit,
        name="prepare",
        cost_estimate=pl.CostEstimate(
            flops=tokens * tokens, bytes_accessed=4 * local_rows * width, transcendentals=0
        ),
    )(
        *(
            pltpu.with_memory_space_constraint(x, pltpu.HBM)
            for x in (sent_lang, block_counts, lang_blocks.T, targets.reshape(1, -1), embedding)
        )
    )
    stats = pl.pallas_call(
        stats_kernel,
        out_shape=struct((devices, 8, LANES), jnp.float32),
        in_specs=[VMEM] * 4,
        out_specs=VMEM,
        scratch_shapes=[pltpu.VMEM((local_rows, group_tokens), jnp.float32)],
        compiler_params=limit,
        name="stats",
        cost_estimate=pl.CostEstimate(
            flops=2 * local_rows * group_tokens * width,
            bytes_accessed=2 * local_rows * width,
            transcendentals=local_rows * group_tokens,
        ),
    )(bias, target_ids, kept, gathered)
    stats = lax.all_to_all(stats, both, 0, 0, tiled=True)
    loss, grad = pl.pallas_call(
        functools.partial(grad_kernel, order, tok_dev, batch_count),
        out_shape=(struct((1, tok_dev), jnp.float32), struct((own_rows, width), jnp.bfloat16)),
        in_specs=[VMEM] * (4 + batch_count),
        out_specs=(VMEM, VMEM),
        scratch_shapes=[
            pltpu.VMEM((own_rows, tokens), jnp.bfloat16),
            pltpu.VMEM((tokens, width), jnp.bfloat16),
        ],
        name="grad",
        compiler_params=limit,
        cost_estimate=pl.CostEstimate(
            flops=4 * own_rows * tokens * width,
            bytes_accessed=2 * own_rows * width,
            transcendentals=own_rows * tokens,
        ),
    )(stats, bias, target_ids, kept, *pieces)
    return (loss.reshape(tok_dev), grad)


def body(hidden, embedding, block_counts, lang_blocks, sent_lang, targets):
    tok_dev, width = hidden.shape
    vocab_count = lax.axis_size("vocab")
    batch_count = lax.axis_size("batch")
    vocab_index = lax.axis_index("vocab")
    batch_index = lax.axis_index("batch")
    local_rows = embedding.shape[0]
    local_blocks = block_counts.shape[0]
    block_width = local_rows // local_blocks
    own_rows = local_rows // batch_count
    own_blocks = own_rows // block_width
    group_tokens = vocab_count * tok_dev
    order = centre_first(vocab_count)
    both = ("vocab", "batch")
    groups = [[v * batch_count + b for v in order] for b in range(batch_count)]

    copies = jnp.broadcast_to(hidden[None], (vocab_count, tok_dev, width))
    gathered = lax.all_to_all(copies, both, 0, 0, tiled=True, axis_index_groups=groups)
    gathered = gathered.reshape(group_tokens, width)
    pieces = [gathered]
    for step in range(1, batch_count):
        pairs = [(b, b ^ step) for b in range(batch_count)]
        pieces.append(lax.ppermute(gathered, "batch", pairs))
    everyone = jnp.concatenate(pieces, axis=0)

    sources = batch_index ^ jnp.arange(batch_count, dtype=jnp.int32)
    places = jnp.array(order, jnp.int32)
    token_ids = (
        (places[None, :, None] * batch_count + sources[:, None, None]) * tok_dev
        + jnp.arange(tok_dev, dtype=jnp.int32)[None, None, :]
    ).reshape(batch_count, group_tokens)
    target_table = targets.reshape(vocab_count, batch_count, tok_dev)
    target_table = jnp.stack([target_table[v] for v in order], axis=1)
    target_ids = jnp.stack(
        [
            lax.dynamic_index_in_dim(target_table, batch_index ^ step, 0, keepdims=False)
            for step in range(batch_count)
        ]
    ).reshape(batch_count, group_tokens)

    block_ids = vocab_index * local_blocks + jnp.arange(local_blocks, dtype=jnp.int32)
    sentence_lists = lang_blocks[sent_lang]
    member = jnp.any(sentence_lists[:, None, :] == block_ids[None, :, None], axis=2)
    sentence_ids = jnp.arange(sent_lang.shape[0], dtype=jnp.int32)
    sentence_hit = (token_ids // SEQ)[None] == sentence_ids[:, None, None]
    allowed = jnp.any(member[:, :, None, None] & sentence_hit[:, None], axis=0)
    log_sampling = jnp.log(block_counts.astype(jnp.float32))

    own_allowed = allowed[:, 0][:, None, :]
    logits = lax.dot_general(
        embedding, gathered, (((1,), (1,)), ((), ())), preferred_element_type=jnp.float32
    ).reshape(local_blocks, block_width, group_tokens) - log_sampling[:, None, None]
    word_ids = (vocab_index * local_rows + jnp.arange(local_rows, dtype=jnp.int32)).reshape(
        local_blocks, block_width
    )
    is_target = word_ids[:, :, None] == target_ids[0][None, None, :]
    local_peak = jnp.max(jnp.where(own_allowed, logits, masked_fill), axis=(0, 1))
    local_total = jnp.sum(
        jnp.where(own_allowed, jnp.exp(logits - local_peak[None, None, :]), 0.0), axis=(0, 1)
    )
    local_target = jnp.sum(jnp.where(is_target, logits, 0.0), axis=(0, 1))
    blank = jnp.zeros_like(local_peak)
    stats = jnp.stack([local_peak, local_total, local_target] + [blank] * 5)
    stats = jnp.broadcast_to(stats[None], (vocab_count * batch_count,) + stats.shape)
    stats = lax.all_to_all(stats, both, 0, 0, tiled=True)
    stats = stats.reshape(vocab_count, batch_count, 8, group_tokens)
    peak = jnp.max(stats[:, :, 0], axis=0)
    total = jnp.sum(stats[:, :, 1] * jnp.exp(stats[:, :, 0] - peak[None]), axis=0)
    log_total = peak + jnp.log(total)
    target_logit = jnp.sum(stats[:, :, 2], axis=0)
    every_loss = lax.dynamic_index_in_dim(log_total - target_logit, batch_index, 0, keepdims=False)
    my_place = jnp.sum(jnp.where(places == vocab_index, jnp.arange(vocab_count), 0))
    token_loss = lax.dynamic_slice_in_dim(every_loss, my_place * tok_dev, tok_dev, 0)
    ordered = jnp.stack(
        [
            lax.dynamic_index_in_dim(log_total, batch_index ^ step, 0, keepdims=False)
            for step in range(batch_count)
        ]
    ).reshape(-1)

    mine = lax.dynamic_slice_in_dim(embedding, batch_index * own_rows, own_rows, 0)
    my_blocks = batch_index * own_blocks
    my_sampling = lax.dynamic_slice_in_dim(log_sampling, my_blocks, own_blocks, 0)
    my_allowed = lax.dynamic_slice_in_dim(allowed, my_blocks, own_blocks, 0)
    my_allowed = my_allowed.reshape(own_blocks, 1, -1)
    my_words = lax.dynamic_slice_in_dim(word_ids, my_blocks, own_blocks, 0)
    my_logits = lax.dot_general(
        mine, everyone, (((1,), (1,)), ((), ())), preferred_element_type=jnp.float32
    ).reshape(own_blocks, block_width, -1) - my_sampling[:, None, None]
    weights = jnp.where(my_allowed, jnp.exp(my_logits - ordered[None, None, :]), 0.0)
    hits = my_words[:, :, None] == target_ids.reshape(-1)[None, None, :]
    grad_logits = (weights - hits.astype(jnp.float32)).astype(jnp.bfloat16)
    grad_embed = lax.dot_general(
        grad_logits.reshape(own_rows, -1),
        everyone,
        (((1,), (0,)), ((), ())),
        preferred_element_type=jnp.float32,
    ).astype(jnp.bfloat16)
    return (token_loss, grad_embed)


def solution(mesh):
    in_specs = (P(("vocab", "batch"), None), P("vocab", None), P("vocab"), P(), P(), P())
    out_specs = (P(("vocab", "batch")), P(("vocab", "batch"), None))

    def step(hidden, *rest):
        group_tokens = hidden.shape[0] * lax.axis_size("vocab")
        chosen = fused_body if LANES % group_tokens == 0 else body
        return chosen(hidden, *rest)

    return jax.shard_map(step, mesh=mesh, in_specs=in_specs, out_specs=out_specs, check_vma=False)
```

```python
import functools

import jax
import jax.numpy as jnp
from jax import lax
from jax.experimental import pallas as pl
from jax.experimental.pallas import tpu as pltpu
from jax.sharding import PartitionSpec as P


SEQ = 64
LANES = 128
KERNEL_VMEM = 8 * 1024 * 1024


masked_fill = float(jnp.finfo(jnp.float32).min)


def centre_first(count):
    return sorted(range(count), key=lambda i: (abs(2 * (i // 2) - count // 2 + 1), -(i % 2), i))


def iota(shape, axis):
    return lax.broadcasted_iota(jnp.int32, shape, axis)


def contract_last(a, b):
    return lax.dot_general(a, b, (((1,), (1,)), ((), ())), preferred_element_type=jnp.float32)


def prepare_kernel(
    order, tok_dev, batch_count, sent_hbm, count_hbm, lists_hbm, targets_hbm, emb_hbm,
    bias_ref, target_ref, kept_ref, sent_ref, count_ref, lists_ref, targets_ref, sems,
):
    sources = (sent_hbm, count_hbm, lists_hbm, targets_hbm, emb_hbm)
    places = (sent_ref, count_ref, lists_ref, targets_ref, kept_ref)
    fetches = [
        pltpu.make_async_copy(src, dst, sems.at[i])
        for i, (src, dst) in enumerate(zip(sources, places))
    ]
    for fetch in fetches:
        fetch.start()
    vocab_index = lax.axis_index("vocab")
    batch_index = lax.axis_index("batch")
    local_blocks, tokens = bias_ref.shape
    group_tokens = tokens // batch_count
    languages = lists_ref.shape[1]

    lane = iota((1, tokens), 1)
    source = batch_index ^ (lane // group_tokens)
    position = (lane % group_tokens) // tok_dev
    place = jnp.zeros((1, tokens), jnp.int32)
    for j, v in enumerate(order):
        place = jnp.where(position == j, v, place)
    token = (place * batch_count + source) * tok_dev + lane % tok_dev
    sentence = token // SEQ

    for fetch in fetches[:-1]:
        fetch.wait()
    found = jnp.zeros((1, tokens), jnp.float32)
    for start in range(0, tokens, LANES):
        size = min(LANES, tokens - start)
        part = targets_ref[:, start : start + size].astype(jnp.float32)
        eye = iota((size, size), 0) == iota((size, size), 1)
        column = jnp.sum(jnp.where(eye, part, 0.0), axis=1, keepdims=True)
        hit = (iota((size, tokens), 0) + start) == token
        found = found + jnp.sum(jnp.where(hit, column, 0.0), axis=0, keepdims=True)
    target_ref[...] = found.astype(jnp.int32)

    block = iota((local_blocks, 1), 0)
    member = jnp.zeros((local_blocks, languages), jnp.float32)
    counts = jnp.zeros((local_blocks, 1), jnp.float32)
    for k in range(local_blocks):
        listed = jnp.where(lists_ref[...] == vocab_index * local_blocks + k, 1.0, 0.0)
        listed = jnp.max(listed, axis=0, keepdims=True)
        member = jnp.where(block == k, listed, member)
        counts = jnp.where(block == k, count_ref[k].astype(jnp.float32), counts)
    log_counts = jnp.log(counts)
    bias = jnp.full((local_blocks, tokens), jnp.inf, jnp.float32)
    language = iota((local_blocks, languages), 1)
    for s in range(sent_ref.shape[0]):
        picked = jnp.where(language == sent_ref[s], member, 0.0)
        picked = jnp.max(picked, axis=1, keepdims=True)
        bias = jnp.where((sentence == s) & (picked > 0.5), log_counts, bias)
    bias_ref[...] = bias
    fetches[-1].wait()


def stats_kernel(bias_ref, target_ref, emb_ref, rows_ref, stats_ref, logits_ref):
    vocab_index = lax.axis_index("vocab")
    group_tokens = rows_ref.shape[0]
    local_rows = emb_ref.shape[0]
    local_blocks = bias_ref.shape[0]
    block_width = local_rows // local_blocks

    raw = contract_last(emb_ref[...], rows_ref[...])
    own_target = target_ref[:, :group_tokens] - vocab_index * local_rows
    word = iota((block_width, group_tokens), 0)
    aimed = jnp.zeros((block_width, group_tokens), jnp.float32)
    peaks, totals = [], []
    for start in range(0, local_blocks, 2):
        top = None
        for k in range(start, start + 2):
            rows = slice(k * block_width, (k + 1) * block_width)
            cell = bias_ref[k : k + 1, :group_tokens]
            logits = jnp.where(cell < jnp.inf, raw[rows] - cell, -jnp.inf)
            logits_ref[rows, :] = logits
            top = logits if top is None else jnp.maximum(top, logits)
            aimed = jnp.where(word + k * block_width == own_target, logits, aimed)
        peaks.append(jnp.maximum(jnp.max(top, axis=0, keepdims=True), masked_fill))
        rows = slice(start * block_width, (start + 2) * block_width)
        part = jnp.exp(logits_ref[rows, :] - peaks[-1])
        totals.append(jnp.sum(part, axis=0, keepdims=True))
    peak = functools.reduce(jnp.maximum, peaks)
    total = sum(t * jnp.exp(p - peak) for p, t in zip(peaks, totals))
    aimed = jnp.sum(aimed, axis=0, keepdims=True)
    row = iota((2, group_tokens), 0)
    first = jnp.where(row == 0, peak, aimed)
    second = jnp.where(row == 0, total, 0.0)
    for p in range(stats_ref.shape[0]):
        stats_ref[p, :, :group_tokens] = first
        stats_ref[p, :, group_tokens:] = second


def scores_kernel(batch_count, bias_ref, target_ref, emb_ref, *refs):
    row_refs = refs[:batch_count]
    logits_ref, everyone_ref = refs[batch_count:]
    batch_index = lax.axis_index("batch")
    group_tokens = row_refs[0].shape[0]
    own_rows = logits_ref.shape[0]
    block_width = emb_ref.shape[0] // bias_ref.shape[0]
    own_blocks = own_rows // block_width

    for m in range(batch_count):
        everyone_ref[m * group_tokens : (m + 1) * group_tokens, :] = row_refs[m][...]
    mine = emb_ref[pl.ds(pl.multiple_of(batch_index * own_rows, own_rows), own_rows), :]
    raw = contract_last(mine, everyone_ref[...])
    for k in range(own_blocks):
        rows = slice(k * block_width, (k + 1) * block_width)
        cell = bias_ref[pl.ds(batch_index * own_blocks + k, 1), :]
        logits_ref[rows, :] = jnp.where(cell < jnp.inf, raw[rows] - cell, -jnp.inf)


def grad_kernel(
    order, tok_dev, batch_count, stats_ref, target_ref, logits_ref, everyone_ref,
    loss_ref, grad_ref, weight_ref, result_ref, mine_ref, sems,
):
    vocab_index = lax.axis_index("vocab")
    batch_index = lax.axis_index("batch")
    own_rows, tokens = logits_ref.shape
    group_tokens = tokens // batch_count
    width = everyone_ref.shape[1]
    vocab_count = stats_ref.shape[0] // batch_count

    rows = []
    for m in range(batch_count):
        group = batch_index ^ m
        parts = stats_ref[pl.ds(group, vocab_count, stride=batch_count), 0, :]
        peak = jnp.max(parts, axis=0, keepdims=True)
        totals = pltpu.roll(parts, group_tokens, 1)
        total = jnp.sum(totals * jnp.exp(parts - peak), axis=0, keepdims=True)
        log_total = peak + jnp.log(total)
        if m == 0:
            aimed = stats_ref[pl.ds(group, vocab_count, stride=batch_count), 1, :]
            loss = log_total - jnp.sum(aimed, axis=0, keepdims=True)
            my_place = jnp.int32(0)
            for j, v in enumerate(order):
                my_place = jnp.where(vocab_index == v, j, my_place)
            wanted = my_place * tok_dev + iota((tok_dev, LANES), 0)
            chosen = jnp.where(iota((tok_dev, LANES), 1) == wanted, loss, 0.0)
            chosen = jnp.sum(chosen, axis=1, keepdims=True)
            eye = iota((tok_dev, tok_dev), 0) == iota((tok_dev, tok_dev), 1)
            mine_ref[...] = jnp.sum(jnp.where(eye, chosen, 0.0), axis=0, keepdims=True)
            pushes = [pltpu.make_async_copy(mine_ref, loss_ref, sems.at[0])]
            pushes[0].start()
        rows.append(log_total)
    low = iota((1, LANES), 1) < group_tokens
    pairs = [
        jnp.where(low, rows[m], pltpu.roll(rows[m + 1], group_tokens, 1))
        for m in range(0, batch_count, 2)
    ]
    target = target_ref[...] - (vocab_index * batch_count + batch_index) * own_rows
    for i, pair in enumerate(pairs):
        lanes = slice(i * LANES, (i + 1) * LANES)
        weight = jnp.exp(logits_ref[:, lanes] - pair)
        hit = iota((own_rows, LANES), 0) == target[:, lanes]
        weight_ref[:, lanes] = (weight - jnp.where(hit, 1.0, 0.0)).astype(jnp.bfloat16)
    chunks = sems.shape[0] - 1
    chunk = width // chunks
    for c in range(chunks):
        columns = slice(c * chunk, (c + 1) * chunk)
        result_ref[:, columns] = jnp.dot(
            weight_ref[...], everyone_ref[:, columns], preferred_element_type=jnp.float32
        ).astype(result_ref.dtype)
        push = pltpu.make_async_copy(
            result_ref.at[:, columns], grad_ref.at[:, columns], sems.at[c + 1]
        )
        push.start()
        pushes.append(push)
    for push in pushes:
        push.wait()


VMEM = pl.BlockSpec(memory_space=pltpu.VMEM)


def fused_body(hidden, embedding, block_counts, lang_blocks, sent_lang, targets):
    tok_dev, width = hidden.shape
    vocab_count = lax.axis_size("vocab")
    batch_count = lax.axis_size("batch")
    local_rows = embedding.shape[0]
    local_blocks = block_counts.shape[0]
    own_rows = local_rows // batch_count
    group_tokens = vocab_count * tok_dev
    tokens = group_tokens * batch_count
    devices = vocab_count * batch_count
    order = centre_first(vocab_count)
    both = ("vocab", "batch")
    groups = [[v * batch_count + b for v in order] for b in range(batch_count)]
    struct = jax.ShapeDtypeStruct

    copies = jnp.broadcast_to(hidden[None], (vocab_count, tok_dev, width))
    gathered = lax.all_to_all(copies, both, 0, 0, tiled=True, axis_index_groups=groups)
    gathered = gathered.reshape(group_tokens, width)
    limit = pltpu.CompilerParams(vmem_limit_bytes=KERNEL_VMEM)
    bias, target_ids, kept = pl.pallas_call(
        functools.partial(prepare_kernel, order, tok_dev, batch_count),
        out_shape=(
            struct((local_blocks, tokens), jnp.float32),
            struct((1, tokens), jnp.int32),
            struct(embedding.shape, embedding.dtype),
        ),
        in_specs=[pl.BlockSpec(memory_space=pltpu.HBM)] * 5,
        out_specs=(VMEM, VMEM, VMEM),
        scratch_shapes=[
            pltpu.SMEM(sent_lang.shape, jnp.int32),
            pltpu.SMEM(block_counts.shape, jnp.int32),
            pltpu.VMEM(lang_blocks.shape[::-1], jnp.int32),
            pltpu.VMEM((1, tokens), jnp.int32),
            pltpu.SemaphoreType.DMA((5,)),
        ],
        compiler_params=limit,
        name="prepare",
        cost_estimate=pl.CostEstimate(
            flops=tokens * tokens, bytes_accessed=4 * local_rows * width, transcendentals=0
        ),
    )(
        *(
            pltpu.with_memory_space_constraint(x, pltpu.HBM)
            for x in (sent_lang, block_counts, lang_blocks.T, targets.reshape(1, -1), embedding)
        )
    )
    stats = pl.pallas_call(
        stats_kernel,
        out_shape=struct((devices, 2, 2 * group_tokens), jnp.float32),
        in_specs=[VMEM] * 4,
        out_specs=VMEM,
        scratch_shapes=[pltpu.VMEM((local_rows, group_tokens), jnp.float32)],
        compiler_params=limit,
        name="stats",
        cost_estimate=pl.CostEstimate(
            flops=2 * local_rows * group_tokens * width,
            bytes_accessed=2 * local_rows * width,
            transcendentals=local_rows * group_tokens,
        ),
    )(bias, target_ids, kept, gathered)
    stats = lax.all_to_all(stats, both, 0, 0, tiled=True)
    pieces = [gathered]
    step = batch_count // 2
    while step:
        pairs = [(b, b ^ step) for b in range(batch_count)]
        received = [lax.ppermute(piece, "batch", pairs) for piece in pieces]
        pieces = [half for pair in zip(pieces, received) for half in pair]
        step //= 2
    logits, everyone = pl.pallas_call(
        functools.partial(scores_kernel, batch_count),
        out_shape=(
            struct((own_rows, tokens), jnp.float32),
            struct((tokens, width), jnp.bfloat16),
        ),
        in_specs=[VMEM] * (3 + batch_count),
        out_specs=(VMEM, VMEM),
        compiler_params=limit,
        name="scores",
        cost_estimate=pl.CostEstimate(
            flops=2 * own_rows * tokens * width,
            bytes_accessed=2 * own_rows * width,
            transcendentals=0,
        ),
    )(bias, target_ids, kept, *pieces)
    loss, grad = pl.pallas_call(
        functools.partial(grad_kernel, order, tok_dev, batch_count),
        out_shape=(struct((1, tok_dev), jnp.float32), struct((own_rows, width), jnp.bfloat16)),
        in_specs=[VMEM] * 4,
        out_specs=(pl.BlockSpec(memory_space=pl.ANY),) * 2,
        scratch_shapes=[
            pltpu.VMEM((own_rows, tokens), jnp.bfloat16),
            pltpu.VMEM((own_rows, width), jnp.bfloat16),
            pltpu.VMEM((1, tok_dev), jnp.float32),
            pltpu.SemaphoreType.DMA((5,)),
        ],
        compiler_params=limit,
        name="grad",
        cost_estimate=pl.CostEstimate(
            flops=2 * own_rows * tokens * width,
            bytes_accessed=2 * own_rows * width,
            transcendentals=own_rows * tokens,
        ),
    )(stats, target_ids, logits, everyone)
    return (loss.reshape(tok_dev), grad)


def body(hidden, embedding, block_counts, lang_blocks, sent_lang, targets):
    tok_dev, width = hidden.shape
    vocab_count = lax.axis_size("vocab")
    batch_count = lax.axis_size("batch")
    vocab_index = lax.axis_index("vocab")
    batch_index = lax.axis_index("batch")
    local_rows = embedding.shape[0]
    local_blocks = block_counts.shape[0]
    block_width = local_rows // local_blocks
    own_rows = local_rows // batch_count
    own_blocks = own_rows // block_width
    group_tokens = vocab_count * tok_dev
    order = centre_first(vocab_count)
    both = ("vocab", "batch")
    groups = [[v * batch_count + b for v in order] for b in range(batch_count)]

    copies = jnp.broadcast_to(hidden[None], (vocab_count, tok_dev, width))
    gathered = lax.all_to_all(copies, both, 0, 0, tiled=True, axis_index_groups=groups)
    gathered = gathered.reshape(group_tokens, width)
    pieces = [gathered]
    for step in range(1, batch_count):
        pairs = [(b, b ^ step) for b in range(batch_count)]
        pieces.append(lax.ppermute(gathered, "batch", pairs))
    everyone = jnp.concatenate(pieces, axis=0)

    sources = batch_index ^ jnp.arange(batch_count, dtype=jnp.int32)
    places = jnp.array(order, jnp.int32)
    token_ids = (
        (places[None, :, None] * batch_count + sources[:, None, None]) * tok_dev
        + jnp.arange(tok_dev, dtype=jnp.int32)[None, None, :]
    ).reshape(batch_count, group_tokens)
    target_table = targets.reshape(vocab_count, batch_count, tok_dev)
    target_table = jnp.stack([target_table[v] for v in order], axis=1)
    target_ids = jnp.stack(
        [
            lax.dynamic_index_in_dim(target_table, batch_index ^ step, 0, keepdims=False)
            for step in range(batch_count)
        ]
    ).reshape(batch_count, group_tokens)

    block_ids = vocab_index * local_blocks + jnp.arange(local_blocks, dtype=jnp.int32)
    sentence_lists = lang_blocks[sent_lang]
    member = jnp.any(sentence_lists[:, None, :] == block_ids[None, :, None], axis=2)
    sentence_ids = jnp.arange(sent_lang.shape[0], dtype=jnp.int32)
    sentence_hit = (token_ids // SEQ)[None] == sentence_ids[:, None, None]
    allowed = jnp.any(member[:, :, None, None] & sentence_hit[:, None], axis=0)
    log_sampling = jnp.log(block_counts.astype(jnp.float32))

    own_allowed = allowed[:, 0][:, None, :]
    logits = lax.dot_general(
        embedding, gathered, (((1,), (1,)), ((), ())), preferred_element_type=jnp.float32
    ).reshape(local_blocks, block_width, group_tokens) - log_sampling[:, None, None]
    word_ids = (vocab_index * local_rows + jnp.arange(local_rows, dtype=jnp.int32)).reshape(
        local_blocks, block_width
    )
    is_target = word_ids[:, :, None] == target_ids[0][None, None, :]
    local_peak = jnp.max(jnp.where(own_allowed, logits, masked_fill), axis=(0, 1))
    local_total = jnp.sum(
        jnp.where(own_allowed, jnp.exp(logits - local_peak[None, None, :]), 0.0), axis=(0, 1)
    )
    local_target = jnp.sum(jnp.where(is_target, logits, 0.0), axis=(0, 1))
    blank = jnp.zeros_like(local_peak)
    stats = jnp.stack([local_peak, local_total, local_target] + [blank] * 5)
    stats = jnp.broadcast_to(stats[None], (vocab_count * batch_count,) + stats.shape)
    stats = lax.all_to_all(stats, both, 0, 0, tiled=True)
    stats = stats.reshape(vocab_count, batch_count, 8, group_tokens)
    peak = jnp.max(stats[:, :, 0], axis=0)
    total = jnp.sum(stats[:, :, 1] * jnp.exp(stats[:, :, 0] - peak[None]), axis=0)
    log_total = peak + jnp.log(total)
    target_logit = jnp.sum(stats[:, :, 2], axis=0)
    every_loss = lax.dynamic_index_in_dim(log_total - target_logit, batch_index, 0, keepdims=False)
    my_place = jnp.sum(jnp.where(places == vocab_index, jnp.arange(vocab_count), 0))
    token_loss = lax.dynamic_slice_in_dim(every_loss, my_place * tok_dev, tok_dev, 0)
    ordered = jnp.stack(
        [
            lax.dynamic_index_in_dim(log_total, batch_index ^ step, 0, keepdims=False)
            for step in range(batch_count)
        ]
    ).reshape(-1)

    mine = lax.dynamic_slice_in_dim(embedding, batch_index * own_rows, own_rows, 0)
    my_blocks = batch_index * own_blocks
    my_sampling = lax.dynamic_slice_in_dim(log_sampling, my_blocks, own_blocks, 0)
    my_allowed = lax.dynamic_slice_in_dim(allowed, my_blocks, own_blocks, 0)
    my_allowed = my_allowed.reshape(own_blocks, 1, -1)
    my_words = lax.dynamic_slice_in_dim(word_ids, my_blocks, own_blocks, 0)
    my_logits = lax.dot_general(
        mine, everyone, (((1,), (1,)), ((), ())), preferred_element_type=jnp.float32
    ).reshape(own_blocks, block_width, -1) - my_sampling[:, None, None]
    weights = jnp.where(my_allowed, jnp.exp(my_logits - ordered[None, None, :]), 0.0)
    hits = my_words[:, :, None] == target_ids.reshape(-1)[None, None, :]
    grad_logits = (weights - hits.astype(jnp.float32)).astype(jnp.bfloat16)
    grad_embed = lax.dot_general(
        grad_logits.reshape(own_rows, -1),
        everyone,
        (((1,), (0,)), ((), ())),
        preferred_element_type=jnp.float32,
    ).astype(jnp.bfloat16)
    return (token_loss, grad_embed)


def solution(mesh):
    in_specs = (P(("vocab", "batch"), None), P("vocab", None), P("vocab"), P(), P(), P())
    out_specs = (P(("vocab", "batch")), P(("vocab", "batch"), None))

    def step(hidden, *rest):
        group_tokens = hidden.shape[0] * lax.axis_size("vocab")
        chosen = fused_body if 2 * group_tokens == LANES else body
        return chosen(hidden, *rest)

    return jax.shard_map(
        step, mesh=mesh, in_specs=in_specs, out_specs=out_specs, check_vma=False
    )
```

```python
import functools

import jax
import jax.numpy as jnp
from jax import lax
from jax.experimental import pallas as pl
from jax.experimental.pallas import tpu as pltpu
from jax.sharding import PartitionSpec as P


SEQ = 64
LANES = 128
KERNEL_VMEM = 8 * 1024 * 1024


masked_fill = float(jnp.finfo(jnp.float32).min)


def centre_first(count):
    return sorted(range(count), key=lambda i: (abs(2 * (i // 2) - count // 2 + 1), -(i % 2), i))


def twist(place, count):
    return place // (count // 2)


def iota(shape, axis):
    return lax.broadcasted_iota(jnp.int32, shape, axis)


def contract_last(a, b):
    return lax.dot_general(a, b, (((1,), (1,)), ((), ())), preferred_element_type=jnp.float32)


def prepare_kernel(
    order, tok_dev, batch_count, sent_hbm, count_hbm, lists_hbm, targets_hbm, emb_hbm,
    bias_ref, target_ref, kept_ref, sent_ref, count_ref, lists_ref, targets_ref, sems,
):
    sources = (sent_hbm, count_hbm, lists_hbm, targets_hbm, emb_hbm)
    places = (sent_ref, count_ref, lists_ref, targets_ref, kept_ref)
    fetches = [
        pltpu.make_async_copy(src, dst, sems.at[i])
        for i, (src, dst) in enumerate(zip(sources, places))
    ]
    for fetch in fetches:
        fetch.start()
    vocab_index = lax.axis_index("vocab")
    batch_index = lax.axis_index("batch")
    local_blocks, tokens = bias_ref.shape
    group_tokens = tokens // batch_count
    vocab_count = group_tokens // tok_dev
    languages = lists_ref.shape[1]

    lane = iota((1, tokens), 1)
    position = (lane % group_tokens) // tok_dev
    place = jnp.zeros((1, tokens), jnp.int32)
    for j, v in enumerate(order):
        place = jnp.where(position == j, v, place)
    twists = twist(place, vocab_count) ^ twist(vocab_index, vocab_count)
    source = batch_index ^ (lane // group_tokens) ^ twists
    token = (place * batch_count + source) * tok_dev + lane % tok_dev
    sentence = token // SEQ

    for fetch in fetches[:-1]:
        fetch.wait()
    found = jnp.zeros((1, tokens), jnp.float32)
    for start in range(0, tokens, LANES):
        size = min(LANES, tokens - start)
        part = targets_ref[:, start : start + size].astype(jnp.float32)
        eye = iota((size, size), 0) == iota((size, size), 1)
        column = jnp.sum(jnp.where(eye, part, 0.0), axis=1, keepdims=True)
        hit = (iota((size, tokens), 0) + start) == token
        found = found + jnp.sum(jnp.where(hit, column, 0.0), axis=0, keepdims=True)
    target_ref[...] = found.astype(jnp.int32)

    block = iota((local_blocks, 1), 0)
    member = jnp.zeros((local_blocks, languages), jnp.float32)
    counts = jnp.zeros((local_blocks, 1), jnp.float32)
    for k in range(local_blocks):
        listed = jnp.where(lists_ref[...] == vocab_index * local_blocks + k, 1.0, 0.0)
        listed = jnp.max(listed, axis=0, keepdims=True)
        member = jnp.where(block == k, listed, member)
        counts = jnp.where(block == k, count_ref[k].astype(jnp.float32), counts)
    log_counts = jnp.log(counts)
    bias = jnp.full((local_blocks, tokens), jnp.inf, jnp.float32)
    language = iota((local_blocks, languages), 1)
    for s in range(sent_ref.shape[0]):
        picked = jnp.where(language == sent_ref[s], member, 0.0)
        picked = jnp.max(picked, axis=1, keepdims=True)
        bias = jnp.where((sentence == s) & (picked > 0.5), log_counts, bias)
    bias_ref[...] = bias
    fetches[-1].wait()


def stats_kernel(bias_ref, target_ref, emb_ref, rows_ref, stats_ref, logits_ref):
    vocab_index = lax.axis_index("vocab")
    group_tokens = rows_ref.shape[0]
    local_rows = emb_ref.shape[0]
    local_blocks = bias_ref.shape[0]
    block_width = local_rows // local_blocks

    raw = contract_last(emb_ref[...], rows_ref[...])
    own_target = target_ref[:, :group_tokens] - vocab_index * local_rows
    word = iota((block_width, group_tokens), 0)
    aimed = jnp.zeros((block_width, group_tokens), jnp.float32)
    peaks, totals = [], []
    for start in range(0, local_blocks, 2):
        top = None
        for k in range(start, start + 2):
            rows = slice(k * block_width, (k + 1) * block_width)
            cell = bias_ref[k : k + 1, :group_tokens]
            logits = jnp.where(cell < jnp.inf, raw[rows] - cell, -jnp.inf)
            logits_ref[rows, :] = logits
            top = logits if top is None else jnp.maximum(top, logits)
            aimed = jnp.where(word + k * block_width == own_target, logits, aimed)
        peaks.append(jnp.maximum(jnp.max(top, axis=0, keepdims=True), masked_fill))
        rows = slice(start * block_width, (start + 2) * block_width)
        part = jnp.exp(logits_ref[rows, :] - peaks[-1])
        totals.append(jnp.sum(part, axis=0, keepdims=True))
    peak = functools.reduce(jnp.maximum, peaks)
    total = sum(t * jnp.exp(p - peak) for p, t in zip(peaks, totals))
    aimed = jnp.sum(aimed, axis=0, keepdims=True)
    row = iota((2, group_tokens), 0)
    first = jnp.where(row == 0, peak, aimed)
    second = jnp.where(row == 0, total, 0.0)
    for p in range(stats_ref.shape[0]):
        stats_ref[p, :, :group_tokens] = first
        stats_ref[p, :, group_tokens:] = second


def scores_kernel(batch_count, bias_ref, target_ref, emb_ref, *refs):
    row_refs = refs[:batch_count]
    logits_ref, everyone_ref = refs[batch_count:]
    batch_index = lax.axis_index("batch")
    group_tokens = row_refs[0].shape[0]
    own_rows = logits_ref.shape[0]
    block_width = emb_ref.shape[0] // bias_ref.shape[0]
    own_blocks = own_rows // block_width

    for m in range(batch_count):
        everyone_ref[m * group_tokens : (m + 1) * group_tokens, :] = row_refs[m][...]
    mine = emb_ref[pl.ds(pl.multiple_of(batch_index * own_rows, own_rows), own_rows), :]
    raw = contract_last(mine, everyone_ref[...])
    for k in range(own_blocks):
        rows = slice(k * block_width, (k + 1) * block_width)
        cell = bias_ref[pl.ds(batch_index * own_blocks + k, 1), :]
        logits_ref[rows, :] = jnp.where(cell < jnp.inf, raw[rows] - cell, -jnp.inf)


def grad_kernel(
    order, tok_dev, batch_count, stats_ref, target_ref, logits_ref, everyone_ref,
    loss_ref, grad_ref, weight_ref, result_ref, mine_ref, sems,
):
    vocab_index = lax.axis_index("vocab")
    batch_index = lax.axis_index("batch")
    own_rows, tokens = logits_ref.shape
    group_tokens = tokens // batch_count
    width = everyone_ref.shape[1]
    vocab_count = stats_ref.shape[0] // batch_count

    rows = []
    for m in range(batch_count):
        group = batch_index ^ twist(vocab_index, vocab_count) ^ m
        half = vocab_count // 2
        starts = (group, half * batch_count + (group ^ 1))
        halves = [stats_ref[pl.ds(start, half, stride=batch_count), 0, :] for start in starts]
        peaks = [jnp.max(parts, axis=0, keepdims=True) for parts in halves]
        peak = jnp.maximum(*peaks)
        total = jnp.zeros_like(peak)
        for parts in halves:
            totals = pltpu.roll(parts, group_tokens, 1)
            total = total + jnp.sum(totals * jnp.exp(parts - peak), axis=0, keepdims=True)
        log_total = peak + jnp.log(total)
        if m == 0:
            loss = log_total
            for start in starts:
                aimed = stats_ref[pl.ds(start, half, stride=batch_count), 1, :]
                loss = loss - jnp.sum(aimed, axis=0, keepdims=True)
            my_place = jnp.int32(0)
            for j, v in enumerate(order):
                my_place = jnp.where(vocab_index == v, j, my_place)
            wanted = my_place * tok_dev + iota((tok_dev, LANES), 0)
            chosen = jnp.where(iota((tok_dev, LANES), 1) == wanted, loss, 0.0)
            chosen = jnp.sum(chosen, axis=1, keepdims=True)
            eye = iota((tok_dev, tok_dev), 0) == iota((tok_dev, tok_dev), 1)
            mine_ref[...] = jnp.sum(jnp.where(eye, chosen, 0.0), axis=0, keepdims=True)
            pushes = [pltpu.make_async_copy(mine_ref, loss_ref, sems.at[0])]
            pushes[0].start()
        rows.append(log_total)
    low = iota((1, LANES), 1) < group_tokens
    pairs = [
        jnp.where(low, rows[m], pltpu.roll(rows[m + 1], group_tokens, 1))
        for m in range(0, batch_count, 2)
    ]
    target = target_ref[...] - (vocab_index * batch_count + batch_index) * own_rows
    for i, pair in enumerate(pairs):
        lanes = slice(i * LANES, (i + 1) * LANES)
        weight = jnp.exp(logits_ref[:, lanes] - pair)
        hit = iota((own_rows, LANES), 0) == target[:, lanes]
        weight_ref[:, lanes] = (weight - jnp.where(hit, 1.0, 0.0)).astype(jnp.bfloat16)
    chunks = sems.shape[0] - 1
    chunk = width // chunks
    for c in range(chunks):
        columns = slice(c * chunk, (c + 1) * chunk)
        result_ref[:, columns] = jnp.dot(
            weight_ref[...], everyone_ref[:, columns], preferred_element_type=jnp.float32
        ).astype(result_ref.dtype)
        push = pltpu.make_async_copy(
            result_ref.at[:, columns], grad_ref.at[:, columns], sems.at[c + 1]
        )
        push.start()
        pushes.append(push)
    for push in pushes:
        push.wait()


VMEM = pl.BlockSpec(memory_space=pltpu.VMEM)


def fused_body(hidden, embedding, block_counts, lang_blocks, sent_lang, targets):
    tok_dev, width = hidden.shape
    vocab_count = lax.axis_size("vocab")
    batch_count = lax.axis_size("batch")
    local_rows = embedding.shape[0]
    local_blocks = block_counts.shape[0]
    own_rows = local_rows // batch_count
    group_tokens = vocab_count * tok_dev
    tokens = group_tokens * batch_count
    devices = vocab_count * batch_count
    order = centre_first(vocab_count)
    both = ("vocab", "batch")
    groups = [
        [v * batch_count + (b ^ twist(v, vocab_count)) for v in order] for b in range(batch_count)
    ]
    struct = jax.ShapeDtypeStruct

    copies = jnp.broadcast_to(hidden[None], (vocab_count, tok_dev, width))
    gathered = lax.all_to_all(copies, both, 0, 0, tiled=True, axis_index_groups=groups)
    gathered = gathered.reshape(group_tokens, width)
    limit = pltpu.CompilerParams(vmem_limit_bytes=KERNEL_VMEM)
    bias, target_ids, kept = pl.pallas_call(
        functools.partial(prepare_kernel, order, tok_dev, batch_count),
        out_shape=(
            struct((local_blocks, tokens), jnp.float32),
            struct((1, tokens), jnp.int32),
            struct(embedding.shape, embedding.dtype),
        ),
        in_specs=[pl.BlockSpec(memory_space=pltpu.HBM)] * 5,
        out_specs=(VMEM, VMEM, VMEM),
        scratch_shapes=[
            pltpu.SMEM(sent_lang.shape, jnp.int32),
            pltpu.SMEM(block_counts.shape, jnp.int32),
            pltpu.VMEM(lang_blocks.shape[::-1], jnp.int32),
            pltpu.VMEM((1, tokens), jnp.int32),
            pltpu.SemaphoreType.DMA((5,)),
        ],
        compiler_params=limit,
        name="prepare",
        cost_estimate=pl.CostEstimate(
            flops=tokens * tokens, bytes_accessed=4 * local_rows * width, transcendentals=0
        ),
    )(
        *(
            pltpu.with_memory_space_constraint(x, pltpu.HBM)
            for x in (sent_lang, block_counts, lang_blocks.T, targets.reshape(1, -1), embedding)
        )
    )
    stats = pl.pallas_call(
        stats_kernel,
        out_shape=struct((devices, 2, 2 * group_tokens), jnp.float32),
        in_specs=[VMEM] * 4,
        out_specs=VMEM,
        scratch_shapes=[pltpu.VMEM((local_rows, group_tokens), jnp.float32)],
        compiler_params=limit,
        name="stats",
        cost_estimate=pl.CostEstimate(
            flops=2 * local_rows * group_tokens * width,
            bytes_accessed=2 * local_rows * width,
            transcendentals=local_rows * group_tokens,
        ),
    )(bias, target_ids, kept, gathered)
    stats = lax.all_to_all(stats, both, 0, 0, tiled=True)
    pieces = [gathered]
    step = batch_count // 2
    while step:
        pairs = [(b, b ^ step) for b in range(batch_count)]
        received = [lax.ppermute(piece, "batch", pairs) for piece in pieces]
        pieces = [half for pair in zip(pieces, received) for half in pair]
        step //= 2
    logits, everyone = pl.pallas_call(
        functools.partial(scores_kernel, batch_count),
        out_shape=(
            struct((own_rows, tokens), jnp.float32),
            struct((tokens, width), jnp.bfloat16),
        ),
        in_specs=[VMEM] * (3 + batch_count),
        out_specs=(VMEM, VMEM),
        compiler_params=limit,
        name="scores",
        cost_estimate=pl.CostEstimate(
            flops=2 * own_rows * tokens * width,
            bytes_accessed=2 * own_rows * width,
            transcendentals=0,
        ),
    )(bias, target_ids, kept, *pieces)
    loss, grad = pl.pallas_call(
        functools.partial(grad_kernel, order, tok_dev, batch_count),
        out_shape=(struct((1, tok_dev), jnp.float32), struct((own_rows, width), jnp.bfloat16)),
        in_specs=[VMEM] * 4,
        out_specs=(pl.BlockSpec(memory_space=pl.ANY),) * 2,
        scratch_shapes=[
            pltpu.VMEM((own_rows, tokens), jnp.bfloat16),
            pltpu.VMEM((own_rows, width), jnp.bfloat16),
            pltpu.VMEM((1, tok_dev), jnp.float32),
            pltpu.SemaphoreType.DMA((5,)),
        ],
        compiler_params=limit,
        name="grad",
        cost_estimate=pl.CostEstimate(
            flops=2 * own_rows * tokens * width,
            bytes_accessed=2 * own_rows * width,
            transcendentals=own_rows * tokens,
        ),
    )(stats, target_ids, logits, everyone)
    return (loss.reshape(tok_dev), grad)


def body(hidden, embedding, block_counts, lang_blocks, sent_lang, targets):
    tok_dev, width = hidden.shape
    vocab_count = lax.axis_size("vocab")
    batch_count = lax.axis_size("batch")
    vocab_index = lax.axis_index("vocab")
    batch_index = lax.axis_index("batch")
    local_rows = embedding.shape[0]
    local_blocks = block_counts.shape[0]
    block_width = local_rows // local_blocks
    own_rows = local_rows // batch_count
    own_blocks = own_rows // block_width
    group_tokens = vocab_count * tok_dev
    order = centre_first(vocab_count)
    both = ("vocab", "batch")
    groups = [[v * batch_count + b for v in order] for b in range(batch_count)]

    copies = jnp.broadcast_to(hidden[None], (vocab_count, tok_dev, width))
    gathered = lax.all_to_all(copies, both, 0, 0, tiled=True, axis_index_groups=groups)
    gathered = gathered.reshape(group_tokens, width)
    pieces = [gathered]
    for step in range(1, batch_count):
        pairs = [(b, b ^ step) for b in range(batch_count)]
        pieces.append(lax.ppermute(gathered, "batch", pairs))
    everyone = jnp.concatenate(pieces, axis=0)

    sources = batch_index ^ jnp.arange(batch_count, dtype=jnp.int32)
    places = jnp.array(order, jnp.int32)
    token_ids = (
        (places[None, :, None] * batch_count + sources[:, None, None]) * tok_dev
        + jnp.arange(tok_dev, dtype=jnp.int32)[None, None, :]
    ).reshape(batch_count, group_tokens)
    target_table = targets.reshape(vocab_count, batch_count, tok_dev)
    target_table = jnp.stack([target_table[v] for v in order], axis=1)
    target_ids = jnp.stack(
        [
            lax.dynamic_index_in_dim(target_table, batch_index ^ step, 0, keepdims=False)
            for step in range(batch_count)
        ]
    ).reshape(batch_count, group_tokens)

    block_ids = vocab_index * local_blocks + jnp.arange(local_blocks, dtype=jnp.int32)
    sentence_lists = lang_blocks[sent_lang]
    member = jnp.any(sentence_lists[:, None, :] == block_ids[None, :, None], axis=2)
    sentence_ids = jnp.arange(sent_lang.shape[0], dtype=jnp.int32)
    sentence_hit = (token_ids // SEQ)[None] == sentence_ids[:, None, None]
    allowed = jnp.any(member[:, :, None, None] & sentence_hit[:, None], axis=0)
    log_sampling = jnp.log(block_counts.astype(jnp.float32))

    own_allowed = allowed[:, 0][:, None, :]
    logits = lax.dot_general(
        embedding, gathered, (((1,), (1,)), ((), ())), preferred_element_type=jnp.float32
    ).reshape(local_blocks, block_width, group_tokens) - log_sampling[:, None, None]
    word_ids = (vocab_index * local_rows + jnp.arange(local_rows, dtype=jnp.int32)).reshape(
        local_blocks, block_width
    )
    is_target = word_ids[:, :, None] == target_ids[0][None, None, :]
    local_peak = jnp.max(jnp.where(own_allowed, logits, masked_fill), axis=(0, 1))
    local_total = jnp.sum(
        jnp.where(own_allowed, jnp.exp(logits - local_peak[None, None, :]), 0.0), axis=(0, 1)
    )
    local_target = jnp.sum(jnp.where(is_target, logits, 0.0), axis=(0, 1))
    blank = jnp.zeros_like(local_peak)
    stats = jnp.stack([local_peak, local_total, local_target] + [blank] * 5)
    stats = jnp.broadcast_to(stats[None], (vocab_count * batch_count,) + stats.shape)
    stats = lax.all_to_all(stats, both, 0, 0, tiled=True)
    stats = stats.reshape(vocab_count, batch_count, 8, group_tokens)
    peak = jnp.max(stats[:, :, 0], axis=0)
    total = jnp.sum(stats[:, :, 1] * jnp.exp(stats[:, :, 0] - peak[None]), axis=0)
    log_total = peak + jnp.log(total)
    target_logit = jnp.sum(stats[:, :, 2], axis=0)
    every_loss = lax.dynamic_index_in_dim(log_total - target_logit, batch_index, 0, keepdims=False)
    my_place = jnp.sum(jnp.where(places == vocab_index, jnp.arange(vocab_count), 0))
    token_loss = lax.dynamic_slice_in_dim(every_loss, my_place * tok_dev, tok_dev, 0)
    ordered = jnp.stack(
        [
            lax.dynamic_index_in_dim(log_total, batch_index ^ step, 0, keepdims=False)
            for step in range(batch_count)
        ]
    ).reshape(-1)

    mine = lax.dynamic_slice_in_dim(embedding, batch_index * own_rows, own_rows, 0)
    my_blocks = batch_index * own_blocks
    my_sampling = lax.dynamic_slice_in_dim(log_sampling, my_blocks, own_blocks, 0)
    my_allowed = lax.dynamic_slice_in_dim(allowed, my_blocks, own_blocks, 0)
    my_allowed = my_allowed.reshape(own_blocks, 1, -1)
    my_words = lax.dynamic_slice_in_dim(word_ids, my_blocks, own_blocks, 0)
    my_logits = lax.dot_general(
        mine, everyone, (((1,), (1,)), ((), ())), preferred_element_type=jnp.float32
    ).reshape(own_blocks, block_width, -1) - my_sampling[:, None, None]
    weights = jnp.where(my_allowed, jnp.exp(my_logits - ordered[None, None, :]), 0.0)
    hits = my_words[:, :, None] == target_ids.reshape(-1)[None, None, :]
    grad_logits = (weights - hits.astype(jnp.float32)).astype(jnp.bfloat16)
    grad_embed = lax.dot_general(
        grad_logits.reshape(own_rows, -1),
        everyone,
        (((1,), (0,)), ((), ())),
        preferred_element_type=jnp.float32,
    ).astype(jnp.bfloat16)
    return (token_loss, grad_embed)


def solution(mesh):
    in_specs = (P(("vocab", "batch"), None), P("vocab", None), P("vocab"), P(), P(), P())
    out_specs = (P(("vocab", "batch")), P(("vocab", "batch"), None))

    def step(hidden, *rest):
        group_tokens = hidden.shape[0] * lax.axis_size("vocab")
        chosen = fused_body if 2 * group_tokens == LANES else body
        return chosen(hidden, *rest)

    return jax.shard_map(
        step, mesh=mesh, in_specs=in_specs, out_specs=out_specs, check_vma=False
    )
```

```python
import functools

import jax
import jax.numpy as jnp
from jax import lax
from jax.experimental import pallas as pl
from jax.experimental.pallas import tpu as pltpu
from jax.sharding import PartitionSpec as P


SEQ = 64
LANES = 128
KERNEL_VMEM = 8 * 1024 * 1024


masked_fill = float(jnp.finfo(jnp.float32).min)


def centre_first(count):
    return sorted(range(count), key=lambda i: (abs(2 * (i // 2) - count // 2 + 1), -(i % 2), i))


def twist(place, count):
    return place // (count // 2)


def iota(shape, axis):
    return lax.broadcasted_iota(jnp.int32, shape, axis)


def contract_last(a, b):
    return lax.dot_general(a, b, (((1,), (1,)), ((), ())), preferred_element_type=jnp.float32)


def prepare_kernel(
    order, tok_dev, batch_count, sent_hbm, count_hbm, lists_hbm, targets_hbm, emb_hbm,
    bias_ref, target_ref, kept_ref, sent_ref, count_ref, lists_ref, targets_ref, sems,
):
    sources = (sent_hbm, count_hbm, lists_hbm, targets_hbm, emb_hbm)
    places = (sent_ref, count_ref, lists_ref, targets_ref, kept_ref)
    fetches = [
        pltpu.make_async_copy(src, dst, sems.at[i])
        for i, (src, dst) in enumerate(zip(sources, places))
    ]
    for fetch in fetches:
        fetch.start()
    vocab_index = lax.axis_index("vocab")
    batch_index = lax.axis_index("batch")
    local_blocks, tokens = bias_ref.shape
    group_tokens = tokens // batch_count
    vocab_count = group_tokens // tok_dev
    languages = lists_ref.shape[1]

    lane = iota((1, tokens), 1)
    position = (lane % group_tokens) // tok_dev
    place = jnp.zeros((1, tokens), jnp.int32)
    for j, v in enumerate(order):
        place = jnp.where(position == j, v, place)
    twists = twist(place, vocab_count) ^ twist(vocab_index, vocab_count)
    source = batch_index ^ (lane // group_tokens) ^ twists
    token = (place * batch_count + source) * tok_dev + lane % tok_dev
    sentence = token // SEQ

    for fetch in fetches[:-1]:
        fetch.wait()
    found = jnp.zeros((1, tokens), jnp.float32)
    for start in range(0, tokens, LANES):
        size = min(LANES, tokens - start)
        part = targets_ref[:, start : start + size].astype(jnp.float32)
        eye = iota((size, size), 0) == iota((size, size), 1)
        column = jnp.sum(jnp.where(eye, part, 0.0), axis=1, keepdims=True)
        hit = (iota((size, tokens), 0) + start) == token
        found = found + jnp.sum(jnp.where(hit, column, 0.0), axis=0, keepdims=True)
    target_ref[...] = found.astype(jnp.int32)

    block = iota((local_blocks, 1), 0)
    member = jnp.zeros((local_blocks, languages), jnp.float32)
    counts = jnp.zeros((local_blocks, 1), jnp.float32)
    for k in range(local_blocks):
        listed = jnp.where(lists_ref[...] == vocab_index * local_blocks + k, 1.0, 0.0)
        listed = jnp.max(listed, axis=0, keepdims=True)
        member = jnp.where(block == k, listed, member)
        counts = jnp.where(block == k, count_ref[k].astype(jnp.float32), counts)
    log_counts = jnp.log(counts)
    bias = jnp.full((local_blocks, tokens), jnp.inf, jnp.float32)
    language = iota((local_blocks, languages), 1)
    for s in range(sent_ref.shape[0]):
        picked = jnp.where(language == sent_ref[s], member, 0.0)
        picked = jnp.max(picked, axis=1, keepdims=True)
        bias = jnp.where((sentence == s) & (picked > 0.5), log_counts, bias)
    bias_ref[...] = bias
    fetches[-1].wait()


def stats_kernel(bias_ref, target_ref, emb_ref, rows_ref, stats_ref, logits_ref):
    vocab_index = lax.axis_index("vocab")
    group_tokens = rows_ref.shape[0]
    local_rows = emb_ref.shape[0]
    local_blocks = bias_ref.shape[0]
    block_width = local_rows // local_blocks

    raw = contract_last(emb_ref[...], rows_ref[...])
    own_target = target_ref[:, :group_tokens] - vocab_index * local_rows
    word = iota((block_width, group_tokens), 0)
    aimed = jnp.zeros((block_width, group_tokens), jnp.float32)
    peaks, totals = [], []
    for start in range(local_blocks):
        top = None
        for k in range(start, start + 1):
            rows = slice(k * block_width, (k + 1) * block_width)
            cell = bias_ref[k : k + 1, :group_tokens]
            logits = jnp.where(cell < jnp.inf, raw[rows] - cell, -jnp.inf)
            logits_ref[rows, :] = logits
            top = logits if top is None else jnp.maximum(top, logits)
            aimed = jnp.where(word + k * block_width == own_target, logits, aimed)
        peaks.append(jnp.maximum(jnp.max(top, axis=0, keepdims=True), masked_fill))
        rows = slice(start * block_width, (start + 1) * block_width)
        part = jnp.exp(logits_ref[rows, :] - peaks[-1])
        totals.append(jnp.sum(part, axis=0, keepdims=True))
    peak = functools.reduce(jnp.maximum, peaks)
    total = sum(t * jnp.exp(p - peak) for p, t in zip(peaks, totals))
    aimed = jnp.sum(aimed, axis=0, keepdims=True)
    row = iota((2, group_tokens), 0)
    first = jnp.where(row == 0, peak, aimed)
    second = jnp.where(row == 0, total, 0.0)
    for p in range(stats_ref.shape[0]):
        stats_ref[p, :, :group_tokens] = first
        stats_ref[p, :, group_tokens:] = second


def own_part(emb_ref, own_rows):
    start = pl.multiple_of(lax.axis_index("batch") * own_rows, own_rows)
    return emb_ref[pl.ds(start, own_rows), :]


def own_bias(bias_ref, rows, own_rows, block_width):
    first = lax.axis_index("batch") * (own_rows // block_width)
    cells = [bias_ref[pl.ds(first + k, 1), :] for k in range(own_rows // block_width)]
    return jnp.concatenate(
        [jnp.broadcast_to(cell[:, rows], (block_width, rows.stop - rows.start)) for cell in cells]
    )


def masked(raw, cells):
    return jnp.where(cells < jnp.inf, raw - cells, -jnp.inf)


def scores_kernel(bias_ref, emb_ref, *refs):
    row_refs = refs[:-2]
    logits_ref, near_ref = refs[-2:]
    group_tokens = row_refs[0].shape[0]
    own_rows, tokens = logits_ref.shape
    block_width = emb_ref.shape[0] // bias_ref.shape[0]
    for m, row_ref in enumerate(row_refs):
        near_ref[m * group_tokens : (m + 1) * group_tokens, :] = row_ref[...]
    raw = contract_last(own_part(emb_ref, own_rows), near_ref[...])
    logits_ref[...] = masked(raw, own_bias(bias_ref, slice(0, tokens), own_rows, block_width))


def grad_kernel(
    order, tok_dev, batch_count, stats_ref, bias_ref, target_ref, emb_ref, logits_ref, near_ref,
    last_ref, loss_ref, grad_ref, weight_ref, everyone_ref, result_ref, mine_ref, sems,
):
    vocab_index = lax.axis_index("vocab")
    batch_index = lax.axis_index("batch")
    own_rows, near_tokens = logits_ref.shape
    group_tokens, width = last_ref.shape
    tokens = near_tokens + group_tokens
    vocab_count = stats_ref.shape[0] // batch_count
    block_width = emb_ref.shape[0] // bias_ref.shape[0]

    start = pl.multiple_of(batch_index * own_rows, own_rows)
    raw = jnp.concatenate(
        [
            contract_last(emb_ref[pl.ds(start + k, own_rows // 2), :], last_ref[...])
            for k in (0, own_rows // 2)
        ]
    )
    everyone_ref[:near_tokens, :] = near_ref[...]
    everyone_ref[near_tokens:, :] = last_ref[...]
    last = masked(raw, own_bias(bias_ref, slice(near_tokens, tokens), own_rows, block_width))

    rows = []
    for m in range(batch_count):
        group = batch_index ^ twist(vocab_index, vocab_count) ^ m
        half = vocab_count // 2
        starts = (group, half * batch_count + (group ^ 1))
        halves = [stats_ref[pl.ds(start, half, stride=batch_count), 0, :] for start in starts]
        peaks = [jnp.max(parts, axis=0, keepdims=True) for parts in halves]
        peak = jnp.maximum(*peaks)
        total = jnp.zeros_like(peak)
        for parts in halves:
            totals = pltpu.roll(parts, group_tokens, 1)
            total = total + jnp.sum(totals * jnp.exp(parts - peak), axis=0, keepdims=True)
        log_total = peak + jnp.log(total)
        if m == 0:
            loss = log_total
            for start in starts:
                aimed = stats_ref[pl.ds(start, half, stride=batch_count), 1, :]
                loss = loss - jnp.sum(aimed, axis=0, keepdims=True)
            my_place = jnp.int32(0)
            for j, v in enumerate(order):
                my_place = jnp.where(vocab_index == v, j, my_place)
            wanted = my_place * tok_dev + iota((tok_dev, LANES), 0)
            chosen = jnp.where(iota((tok_dev, LANES), 1) == wanted, loss, 0.0)
            chosen = jnp.sum(chosen, axis=1, keepdims=True)
            eye = iota((tok_dev, tok_dev), 0) == iota((tok_dev, tok_dev), 1)
            mine_ref[...] = jnp.sum(jnp.where(eye, chosen, 0.0), axis=0, keepdims=True)
            pushes = [pltpu.make_async_copy(mine_ref, loss_ref, sems.at[0])]
            pushes[0].start()
        rows.append(log_total)
    low = iota((1, LANES), 1) < group_tokens
    pairs = [
        jnp.where(low, rows[m], pltpu.roll(rows[m + 1], group_tokens, 1))
        for m in range(0, batch_count, 2)
    ]
    target = target_ref[...] - (vocab_index * batch_count + batch_index) * own_rows
    for start, stop in ((0, LANES), (LANES, near_tokens), (near_tokens, tokens)):
        lanes = slice(start, stop)
        logits = last if start == near_tokens else logits_ref[:, lanes]
        offset = start % LANES
        log_total = pairs[start // LANES][:, offset : offset + stop - start]
        weight = jnp.exp(logits - log_total)
        hit = iota(logits.shape, 0) == target[:, lanes]
        weight_ref[:, lanes] = (weight - jnp.where(hit, 1.0, 0.0)).astype(jnp.bfloat16)
    chunks = sems.shape[0] - 1
    chunk = width // chunks
    for c in range(chunks):
        columns = slice(c * chunk, (c + 1) * chunk)
        result_ref[:, columns] = jnp.dot(
            weight_ref[...], everyone_ref[:, columns], preferred_element_type=jnp.float32
        ).astype(result_ref.dtype)
        push = pltpu.make_async_copy(
            result_ref.at[:, columns], grad_ref.at[:, columns], sems.at[c + 1]
        )
        push.start()
        pushes.append(push)
    for push in pushes:
        push.wait()


VMEM = pl.BlockSpec(memory_space=pltpu.VMEM)


def fused_body(hidden, embedding, block_counts, lang_blocks, sent_lang, targets):
    tok_dev, width = hidden.shape
    vocab_count = lax.axis_size("vocab")
    batch_count = lax.axis_size("batch")
    local_rows = embedding.shape[0]
    local_blocks = block_counts.shape[0]
    own_rows = local_rows // batch_count
    group_tokens = vocab_count * tok_dev
    tokens = group_tokens * batch_count
    devices = vocab_count * batch_count
    order = centre_first(vocab_count)
    both = ("vocab", "batch")
    groups = [
        [v * batch_count + (b ^ twist(v, vocab_count)) for v in order] for b in range(batch_count)
    ]
    struct = jax.ShapeDtypeStruct

    copies = jnp.broadcast_to(hidden[None], (vocab_count, tok_dev, width))
    gathered = lax.all_to_all(copies, both, 0, 0, tiled=True, axis_index_groups=groups)
    gathered = gathered.reshape(group_tokens, width)
    limit = pltpu.CompilerParams(vmem_limit_bytes=KERNEL_VMEM)
    bias, target_ids, kept = pl.pallas_call(
        functools.partial(prepare_kernel, order, tok_dev, batch_count),
        out_shape=(
            struct((local_blocks, tokens), jnp.float32),
            struct((1, tokens), jnp.int32),
            struct(embedding.shape, embedding.dtype),
        ),
        in_specs=[pl.BlockSpec(memory_space=pltpu.HBM)] * 5,
        out_specs=(VMEM, VMEM, VMEM),
        scratch_shapes=[
            pltpu.SMEM(sent_lang.shape, jnp.int32),
            pltpu.SMEM(block_counts.shape, jnp.int32),
            pltpu.VMEM(lang_blocks.shape[::-1], jnp.int32),
            pltpu.VMEM((1, tokens), jnp.int32),
            pltpu.SemaphoreType.DMA((5,)),
        ],
        compiler_params=limit,
        name="prepare",
        cost_estimate=pl.CostEstimate(
            flops=tokens * tokens, bytes_accessed=4 * local_rows * width, transcendentals=0
        ),
    )(
        *(
            pltpu.with_memory_space_constraint(x, pltpu.HBM)
            for x in (sent_lang, block_counts, lang_blocks.T, targets.reshape(1, -1), embedding)
        )
    )
    stats = pl.pallas_call(
        stats_kernel,
        out_shape=struct((devices, 2, 2 * group_tokens), jnp.float32),
        in_specs=[VMEM] * 4,
        out_specs=VMEM,
        scratch_shapes=[pltpu.VMEM((local_rows, group_tokens), jnp.float32)],
        compiler_params=limit,
        name="stats",
        cost_estimate=pl.CostEstimate(
            flops=2 * local_rows * group_tokens * width,
            bytes_accessed=2 * local_rows * width,
            transcendentals=local_rows * group_tokens,
        ),
    )(bias, target_ids, kept, gathered)
    stats = lax.all_to_all(stats, both, 0, 0, tiled=True)
    pieces = [gathered]
    step = batch_count // 2
    while step:
        pairs = [(b, b ^ step) for b in range(batch_count)]
        received = []
        for piece in pieces:
            received.append(lax.ppermute(piece, "batch", pairs))
        pieces = [half for pair in zip(pieces, received) for half in pair]
        step //= 2
    near_tokens = tokens - group_tokens
    logits, near = pl.pallas_call(
        scores_kernel,
        out_shape=(
            struct((own_rows, near_tokens), jnp.float32),
            struct((near_tokens, width), jnp.bfloat16),
        ),
        in_specs=[VMEM] * (1 + batch_count),
        out_specs=(VMEM, VMEM),
        compiler_params=limit,
        name="scores",
        cost_estimate=pl.CostEstimate(
            flops=2 * own_rows * near_tokens * width,
            bytes_accessed=2 * own_rows * width,
            transcendentals=0,
        ),
    )(bias, kept, *pieces[:-1])
    loss, grad = pl.pallas_call(
        functools.partial(grad_kernel, order, tok_dev, batch_count),
        out_shape=(struct((1, tok_dev), jnp.float32), struct((own_rows, width), jnp.bfloat16)),
        in_specs=[VMEM] * 7,
        out_specs=(pl.BlockSpec(memory_space=pl.ANY),) * 2,
        scratch_shapes=[
            pltpu.VMEM((own_rows, tokens), jnp.bfloat16),
            pltpu.VMEM((tokens, width), jnp.bfloat16),
            pltpu.VMEM((own_rows, width), jnp.bfloat16),
            pltpu.VMEM((1, tok_dev), jnp.float32),
            pltpu.SemaphoreType.DMA((3,)),
        ],
        compiler_params=limit,
        name="grad",
        cost_estimate=pl.CostEstimate(
            flops=2 * own_rows * (tokens + group_tokens) * width,
            bytes_accessed=2 * own_rows * width,
            transcendentals=own_rows * tokens,
        ),
    )(stats, bias, target_ids, kept, logits, near, pieces[-1])
    return (loss.reshape(tok_dev), grad)


def body(hidden, embedding, block_counts, lang_blocks, sent_lang, targets):
    tok_dev, width = hidden.shape
    vocab_count = lax.axis_size("vocab")
    batch_count = lax.axis_size("batch")
    vocab_index = lax.axis_index("vocab")
    batch_index = lax.axis_index("batch")
    local_rows = embedding.shape[0]
    local_blocks = block_counts.shape[0]
    block_width = local_rows // local_blocks
    own_rows = local_rows // batch_count
    own_blocks = own_rows // block_width
    group_tokens = vocab_count * tok_dev
    order = centre_first(vocab_count)
    both = ("vocab", "batch")
    groups = [[v * batch_count + b for v in order] for b in range(batch_count)]

    copies = jnp.broadcast_to(hidden[None], (vocab_count, tok_dev, width))
    gathered = lax.all_to_all(copies, both, 0, 0, tiled=True, axis_index_groups=groups)
    gathered = gathered.reshape(group_tokens, width)
    pieces = [gathered]
    for step in range(1, batch_count):
        pairs = [(b, b ^ step) for b in range(batch_count)]
        pieces.append(lax.ppermute(gathered, "batch", pairs))
    everyone = jnp.concatenate(pieces, axis=0)

    sources = batch_index ^ jnp.arange(batch_count, dtype=jnp.int32)
    places = jnp.array(order, jnp.int32)
    token_ids = (
        (places[None, :, None] * batch_count + sources[:, None, None]) * tok_dev
        + jnp.arange(tok_dev, dtype=jnp.int32)[None, None, :]
    ).reshape(batch_count, group_tokens)
    target_table = targets.reshape(vocab_count, batch_count, tok_dev)
    target_table = jnp.stack([target_table[v] for v in order], axis=1)
    target_ids = jnp.stack(
        [
            lax.dynamic_index_in_dim(target_table, batch_index ^ step, 0, keepdims=False)
            for step in range(batch_count)
        ]
    ).reshape(batch_count, group_tokens)

    block_ids = vocab_index * local_blocks + jnp.arange(local_blocks, dtype=jnp.int32)
    sentence_lists = lang_blocks[sent_lang]
    member = jnp.any(sentence_lists[:, None, :] == block_ids[None, :, None], axis=2)
    sentence_ids = jnp.arange(sent_lang.shape[0], dtype=jnp.int32)
    sentence_hit = (token_ids // SEQ)[None] == sentence_ids[:, None, None]
    allowed = jnp.any(member[:, :, None, None] & sentence_hit[:, None], axis=0)
    log_sampling = jnp.log(block_counts.astype(jnp.float32))

    own_allowed = allowed[:, 0][:, None, :]
    logits = lax.dot_general(
        embedding, gathered, (((1,), (1,)), ((), ())), preferred_element_type=jnp.float32
    ).reshape(local_blocks, block_width, group_tokens) - log_sampling[:, None, None]
    word_ids = (vocab_index * local_rows + jnp.arange(local_rows, dtype=jnp.int32)).reshape(
        local_blocks, block_width
    )
    is_target = word_ids[:, :, None] == target_ids[0][None, None, :]
    local_peak = jnp.max(jnp.where(own_allowed, logits, masked_fill), axis=(0, 1))
    local_total = jnp.sum(
        jnp.where(own_allowed, jnp.exp(logits - local_peak[None, None, :]), 0.0), axis=(0, 1)
    )
    local_target = jnp.sum(jnp.where(is_target, logits, 0.0), axis=(0, 1))
    blank = jnp.zeros_like(local_peak)
    stats = jnp.stack([local_peak, local_total, local_target] + [blank] * 5)
    stats = jnp.broadcast_to(stats[None], (vocab_count * batch_count,) + stats.shape)
    stats = lax.all_to_all(stats, both, 0, 0, tiled=True)
    stats = stats.reshape(vocab_count, batch_count, 8, group_tokens)
    peak = jnp.max(stats[:, :, 0], axis=0)
    total = jnp.sum(stats[:, :, 1] * jnp.exp(stats[:, :, 0] - peak[None]), axis=0)
    log_total = peak + jnp.log(total)
    target_logit = jnp.sum(stats[:, :, 2], axis=0)
    every_loss = lax.dynamic_index_in_dim(log_total - target_logit, batch_index, 0, keepdims=False)
    my_place = jnp.sum(jnp.where(places == vocab_index, jnp.arange(vocab_count), 0))
    token_loss = lax.dynamic_slice_in_dim(every_loss, my_place * tok_dev, tok_dev, 0)
    ordered = jnp.stack(
        [
            lax.dynamic_index_in_dim(log_total, batch_index ^ step, 0, keepdims=False)
            for step in range(batch_count)
        ]
    ).reshape(-1)

    mine = lax.dynamic_slice_in_dim(embedding, batch_index * own_rows, own_rows, 0)
    my_blocks = batch_index * own_blocks
    my_sampling = lax.dynamic_slice_in_dim(log_sampling, my_blocks, own_blocks, 0)
    my_allowed = lax.dynamic_slice_in_dim(allowed, my_blocks, own_blocks, 0)
    my_allowed = my_allowed.reshape(own_blocks, 1, -1)
    my_words = lax.dynamic_slice_in_dim(word_ids, my_blocks, own_blocks, 0)
    my_logits = lax.dot_general(
        mine, everyone, (((1,), (1,)), ((), ())), preferred_element_type=jnp.float32
    ).reshape(own_blocks, block_width, -1) - my_sampling[:, None, None]
    weights = jnp.where(my_allowed, jnp.exp(my_logits - ordered[None, None, :]), 0.0)
    hits = my_words[:, :, None] == target_ids.reshape(-1)[None, None, :]
    grad_logits = (weights - hits.astype(jnp.float32)).astype(jnp.bfloat16)
    grad_embed = lax.dot_general(
        grad_logits.reshape(own_rows, -1),
        everyone,
        (((1,), (0,)), ((), ())),
        preferred_element_type=jnp.float32,
    ).astype(jnp.bfloat16)
    return (token_loss, grad_embed)


def solution(mesh):
    in_specs = (P(("vocab", "batch"), None), P("vocab", None), P("vocab"), P(), P(), P())
    out_specs = (P(("vocab", "batch")), P(("vocab", "batch"), None))

    def step(hidden, *rest):
        group_tokens = hidden.shape[0] * lax.axis_size("vocab")
        chosen = fused_body if (2 * group_tokens, lax.axis_size("batch")) == (LANES, 4) else body
        return chosen(hidden, *rest)

    return jax.shard_map(
        step, mesh=mesh, in_specs=in_specs, out_specs=out_specs, check_vma=False
    )
```

```python
import functools

import jax
import jax.numpy as jnp
from jax import lax
from jax.experimental import pallas as pl
from jax.experimental.pallas import tpu as pltpu
from jax.sharding import PartitionSpec as P


SEQ = 64
LANES = 128
KERNEL_VMEM = 8 * 1024 * 1024


masked_fill = float(jnp.finfo(jnp.float32).min)


def centre_first(count):
    return sorted(range(count), key=lambda i: (abs(2 * (i // 2) - count // 2 + 1), -(i % 2), i))


def twist(place, count):
    return place // (count // 2)


def iota(shape, axis):
    return lax.broadcasted_iota(jnp.int32, shape, axis)


def contract_last(a, b):
    return lax.dot_general(a, b, (((1,), (1,)), ((), ())), preferred_element_type=jnp.float32)


def prepare_kernel(
    order, tok_dev, batch_count, sent_hbm, count_hbm, lists_hbm, targets_hbm, emb_hbm,
    bias_ref, target_ref, kept_ref, sent_ref, count_ref, lists_ref, targets_ref, sems,
):
    sources = (sent_hbm, count_hbm, lists_hbm, targets_hbm, emb_hbm)
    places = (sent_ref, count_ref, lists_ref, targets_ref, kept_ref)
    fetches = [
        pltpu.make_async_copy(src, dst, sems.at[i])
        for i, (src, dst) in enumerate(zip(sources, places))
    ]
    for fetch in fetches:
        fetch.start()
    vocab_index = lax.axis_index("vocab")
    batch_index = lax.axis_index("batch")
    local_blocks, tokens = bias_ref.shape
    group_tokens = tokens // batch_count
    vocab_count = group_tokens // tok_dev
    languages = lists_ref.shape[1]

    lane = iota((1, tokens), 1)
    position = (lane % group_tokens) // tok_dev
    place = jnp.zeros((1, tokens), jnp.int32)
    for j, v in enumerate(order):
        place = jnp.where(position == j, v, place)
    twists = twist(place, vocab_count) ^ twist(vocab_index, vocab_count)
    source = batch_index ^ (lane // group_tokens) ^ twists
    token = (place * batch_count + source) * tok_dev + lane % tok_dev
    sentence = token // SEQ

    for fetch in fetches[:-1]:
        fetch.wait()
    found = jnp.zeros((1, tokens), jnp.float32)
    for start in range(0, tokens, LANES):
        size = min(LANES, tokens - start)
        part = targets_ref[:, start : start + size].astype(jnp.float32)
        eye = iota((size, size), 0) == iota((size, size), 1)
        column = jnp.sum(jnp.where(eye, part, 0.0), axis=1, keepdims=True)
        hit = (iota((size, tokens), 0) + start) == token
        found = found + jnp.sum(jnp.where(hit, column, 0.0), axis=0, keepdims=True)
    target_ref[...] = found.astype(jnp.int32)

    block = iota((local_blocks, 1), 0)
    member = jnp.zeros((local_blocks, languages), jnp.float32)
    counts = jnp.zeros((local_blocks, 1), jnp.float32)
    for k in range(local_blocks):
        listed = jnp.where(lists_ref[...] == vocab_index * local_blocks + k, 1.0, 0.0)
        listed = jnp.max(listed, axis=0, keepdims=True)
        member = jnp.where(block == k, listed, member)
        counts = jnp.where(block == k, count_ref[k].astype(jnp.float32), counts)
    log_counts = jnp.log(counts)
    bias = jnp.full((local_blocks, tokens), jnp.inf, jnp.float32)
    language = iota((local_blocks, languages), 1)
    for s in range(sent_ref.shape[0]):
        picked = jnp.where(language == sent_ref[s], member, 0.0)
        picked = jnp.max(picked, axis=1, keepdims=True)
        bias = jnp.where((sentence == s) & (picked > 0.5), log_counts, bias)
    bias_ref[...] = bias
    fetches[-1].wait()


def stats_kernel(bias_ref, target_ref, emb_ref, rows_ref, stats_ref, logits_ref):
    vocab_index = lax.axis_index("vocab")
    group_tokens = rows_ref.shape[0]
    local_rows = emb_ref.shape[0]
    local_blocks = bias_ref.shape[0]
    block_width = local_rows // local_blocks

    raw = contract_last(emb_ref[...], rows_ref[...])
    own_target = target_ref[:, :group_tokens] - vocab_index * local_rows
    word = iota((block_width, group_tokens), 0)
    aimed = jnp.zeros((block_width, group_tokens), jnp.float32)
    peaks, totals = [], []
    for start in range(0, local_blocks, 2):
        top = None
        for k in range(start, start + 2):
            rows = slice(k * block_width, (k + 1) * block_width)
            cell = bias_ref[k : k + 1, :group_tokens]
            logits = jnp.where(cell < jnp.inf, raw[rows] - cell, -jnp.inf)
            logits_ref[rows, :] = logits
            top = logits if top is None else jnp.maximum(top, logits)
            aimed = jnp.where(word + k * block_width == own_target, logits, aimed)
        peaks.append(jnp.maximum(jnp.max(top, axis=0, keepdims=True), masked_fill))
        rows = slice(start * block_width, (start + 2) * block_width)
        part = jnp.exp(logits_ref[rows, :] - peaks[-1])
        totals.append(jnp.sum(part, axis=0, keepdims=True))
    peak = functools.reduce(jnp.maximum, peaks)
    total = sum(t * jnp.exp(p - peak) for p, t in zip(peaks, totals))
    aimed = jnp.sum(aimed, axis=0, keepdims=True)
    row = iota((2, group_tokens), 0)
    first = jnp.where(row == 0, peak, aimed)
    second = jnp.where(row == 0, total, 0.0)
    for p in range(stats_ref.shape[0]):
        stats_ref[p, :, :group_tokens] = first
        stats_ref[p, :, group_tokens:] = second


def own_part(emb_ref, own_rows):
    start = pl.multiple_of(lax.axis_index("batch") * own_rows, own_rows)
    return emb_ref[pl.ds(start, own_rows), :]


def own_bias(bias_ref, rows, own_rows, block_width):
    first = lax.axis_index("batch") * (own_rows // block_width)
    cells = [bias_ref[pl.ds(first + k, 1), :] for k in range(own_rows // block_width)]
    return jnp.concatenate(
        [jnp.broadcast_to(cell[:, rows], (block_width, rows.stop - rows.start)) for cell in cells]
    )


def masked(raw, cells):
    return jnp.where(cells < jnp.inf, raw - cells, -jnp.inf)


def scores_kernel(bias_ref, emb_ref, *refs):
    row_refs = refs[:-2]
    logits_ref, near_ref = refs[-2:]
    group_tokens = row_refs[0].shape[0]
    own_rows, tokens = logits_ref.shape
    block_width = emb_ref.shape[0] // bias_ref.shape[0]
    for m, row_ref in enumerate(row_refs):
        near_ref[m * group_tokens : (m + 1) * group_tokens, :] = row_ref[...]
    raw = contract_last(own_part(emb_ref, own_rows), near_ref[...])
    logits_ref[...] = masked(raw, own_bias(bias_ref, slice(0, tokens), own_rows, block_width))


def grad_kernel(
    order, tok_dev, batch_count, stats_ref, bias_ref, target_ref, emb_ref, logits_ref, near_ref,
    last_ref, loss_ref, grad_ref, weight_ref, everyone_ref, result_ref, mine_ref, sems,
):
    vocab_index = lax.axis_index("vocab")
    batch_index = lax.axis_index("batch")
    own_rows, near_tokens = logits_ref.shape
    group_tokens, width = last_ref.shape
    tokens = near_tokens + group_tokens
    vocab_count = stats_ref.shape[0] // batch_count
    block_width = emb_ref.shape[0] // bias_ref.shape[0]

    start = pl.multiple_of(batch_index * own_rows, own_rows)
    raw = jnp.concatenate(
        [
            contract_last(emb_ref[pl.ds(start + k, own_rows // 2), :], last_ref[...])
            for k in (0, own_rows // 2)
        ]
    )
    everyone_ref[:near_tokens, :] = near_ref[...]
    everyone_ref[near_tokens:, :] = last_ref[...]
    last = masked(raw, own_bias(bias_ref, slice(near_tokens, tokens), own_rows, block_width))

    rows = []
    for m in range(batch_count):
        group = batch_index ^ twist(vocab_index, vocab_count) ^ m
        half = vocab_count // 2
        starts = (group, half * batch_count + (group ^ 1))
        halves = [stats_ref[pl.ds(start, half, stride=batch_count), 0, :] for start in starts]
        peaks = [jnp.max(parts, axis=0, keepdims=True) for parts in halves]
        peak = jnp.maximum(*peaks)
        total = jnp.zeros_like(peak)
        for parts in halves:
            totals = pltpu.roll(parts, group_tokens, 1)
            total = total + jnp.sum(totals * jnp.exp(parts - peak), axis=0, keepdims=True)
        log_total = peak + jnp.log(total)
        if m == 0:
            loss = log_total
            for start in starts:
                aimed = stats_ref[pl.ds(start, half, stride=batch_count), 1, :]
                loss = loss - jnp.sum(aimed, axis=0, keepdims=True)
            my_place = jnp.int32(0)
            for j, v in enumerate(order):
                my_place = jnp.where(vocab_index == v, j, my_place)
            wanted = my_place * tok_dev + iota((tok_dev, LANES), 0)
            chosen = jnp.where(iota((tok_dev, LANES), 1) == wanted, loss, 0.0)
            chosen = jnp.sum(chosen, axis=1, keepdims=True)
            eye = iota((tok_dev, tok_dev), 0) == iota((tok_dev, tok_dev), 1)
            mine_ref[...] = jnp.sum(jnp.where(eye, chosen, 0.0), axis=0, keepdims=True)
            pushes = [pltpu.make_async_copy(mine_ref, loss_ref, sems.at[0])]
            pushes[0].start()
        rows.append(log_total)
    low = iota((1, LANES), 1) < group_tokens
    pairs = [
        jnp.where(low, rows[m], pltpu.roll(rows[m + 1], group_tokens, 1))
        for m in range(0, batch_count, 2)
    ]
    target = target_ref[...] - (vocab_index * batch_count + batch_index) * own_rows
    for start, stop in ((0, LANES), (LANES, near_tokens), (near_tokens, tokens)):
        lanes = slice(start, stop)
        logits = last if start == near_tokens else logits_ref[:, lanes]
        offset = start % LANES
        log_total = pairs[start // LANES][:, offset : offset + stop - start]
        weight = jnp.exp(logits - log_total)
        hit = iota(logits.shape, 0) == target[:, lanes]
        weight_ref[:, lanes] = (weight - jnp.where(hit, 1.0, 0.0)).astype(jnp.bfloat16)
    chunks = sems.shape[0] - 1
    chunk = width // chunks
    for c in range(chunks):
        columns = slice(c * chunk, (c + 1) * chunk)
        result_ref[:, columns] = jnp.dot(
            weight_ref[...], everyone_ref[:, columns], preferred_element_type=jnp.float32
        ).astype(result_ref.dtype)
        push = pltpu.make_async_copy(
            result_ref.at[:, columns], grad_ref.at[:, columns], sems.at[c + 1]
        )
        push.start()
        pushes.append(push)
    for push in pushes:
        push.wait()


VMEM = pl.BlockSpec(memory_space=pltpu.VMEM)


def fused_body(hidden, embedding, block_counts, lang_blocks, sent_lang, targets):
    tok_dev, width = hidden.shape
    vocab_count = lax.axis_size("vocab")
    batch_count = lax.axis_size("batch")
    local_rows = embedding.shape[0]
    local_blocks = block_counts.shape[0]
    own_rows = local_rows // batch_count
    group_tokens = vocab_count * tok_dev
    tokens = group_tokens * batch_count
    devices = vocab_count * batch_count
    order = centre_first(vocab_count)
    both = ("vocab", "batch")
    groups = [
        [v * batch_count + (b ^ twist(v, vocab_count)) for v in order] for b in range(batch_count)
    ]
    struct = jax.ShapeDtypeStruct

    copies = jnp.broadcast_to(hidden[None], (vocab_count, tok_dev, width))
    gathered = lax.all_to_all(copies, both, 0, 0, tiled=True, axis_index_groups=groups)
    gathered = gathered.reshape(group_tokens, width)
    limit = pltpu.CompilerParams(vmem_limit_bytes=KERNEL_VMEM)
    bias, target_ids, kept = pl.pallas_call(
        functools.partial(prepare_kernel, order, tok_dev, batch_count),
        out_shape=(
            struct((local_blocks, tokens), jnp.float32),
            struct((1, tokens), jnp.int32),
            struct(embedding.shape, embedding.dtype),
        ),
        in_specs=[pl.BlockSpec(memory_space=pltpu.HBM)] * 5,
        out_specs=(VMEM, VMEM, VMEM),
        scratch_shapes=[
            pltpu.SMEM(sent_lang.shape, jnp.int32),
            pltpu.SMEM(block_counts.shape, jnp.int32),
            pltpu.VMEM(lang_blocks.shape[::-1], jnp.int32),
            pltpu.VMEM((1, tokens), jnp.int32),
            pltpu.SemaphoreType.DMA((5,)),
        ],
        compiler_params=limit,
        name="prepare",
        cost_estimate=pl.CostEstimate(
            flops=tokens * tokens, bytes_accessed=4 * local_rows * width, transcendentals=0
        ),
    )(
        *(
            pltpu.with_memory_space_constraint(x, pltpu.HBM)
            for x in (sent_lang, block_counts, lang_blocks.T, targets.reshape(1, -1), embedding)
        )
    )
    stats = pl.pallas_call(
        stats_kernel,
        out_shape=struct((devices, 2, 2 * group_tokens), jnp.float32),
        in_specs=[VMEM] * 4,
        out_specs=VMEM,
        scratch_shapes=[pltpu.VMEM((local_rows, group_tokens), jnp.float32)],
        compiler_params=limit,
        name="stats",
        cost_estimate=pl.CostEstimate(
            flops=2 * local_rows * group_tokens * width,
            bytes_accessed=2 * local_rows * width,
            transcendentals=local_rows * group_tokens,
        ),
    )(bias, target_ids, kept, gathered)
    stats = lax.all_to_all(stats, both, 0, 0, tiled=True)
    pieces = [gathered]
    step = batch_count // 2
    while step:
        pairs = [(b, b ^ step) for b in range(batch_count)]
        received = []
        for piece in pieces:
            received.append(lax.ppermute(piece, "batch", pairs))
        pieces = [half for pair in zip(pieces, received) for half in pair]
        step //= 2
    near_tokens = tokens - group_tokens
    logits, near = pl.pallas_call(
        scores_kernel,
        out_shape=(
            struct((own_rows, near_tokens), jnp.float32),
            struct((near_tokens, width), jnp.bfloat16),
        ),
        in_specs=[VMEM] * (1 + batch_count),
        out_specs=(VMEM, VMEM),
        compiler_params=limit,
        name="scores",
        cost_estimate=pl.CostEstimate(
            flops=2 * own_rows * near_tokens * width,
            bytes_accessed=2 * own_rows * width,
            transcendentals=0,
        ),
    )(bias, kept, *pieces[:-1])
    loss, grad = pl.pallas_call(
        functools.partial(grad_kernel, order, tok_dev, batch_count),
        out_shape=(struct((1, tok_dev), jnp.float32), struct((own_rows, width), jnp.bfloat16)),
        in_specs=[VMEM] * 7,
        out_specs=(pl.BlockSpec(memory_space=pl.ANY),) * 2,
        scratch_shapes=[
            pltpu.VMEM((own_rows, tokens), jnp.bfloat16),
            pltpu.VMEM((tokens, width), jnp.bfloat16),
            pltpu.VMEM((own_rows, width), jnp.bfloat16),
            pltpu.VMEM((1, tok_dev), jnp.float32),
            pltpu.SemaphoreType.DMA((5,)),
        ],
        compiler_params=limit,
        name="grad",
        cost_estimate=pl.CostEstimate(
            flops=2 * own_rows * (tokens + group_tokens) * width,
            bytes_accessed=2 * own_rows * width,
            transcendentals=own_rows * tokens,
        ),
    )(stats, bias, target_ids, kept, logits, near, pieces[-1])
    return (loss.reshape(tok_dev), grad)


def body(hidden, embedding, block_counts, lang_blocks, sent_lang, targets):
    tok_dev, width = hidden.shape
    vocab_count = lax.axis_size("vocab")
    batch_count = lax.axis_size("batch")
    vocab_index = lax.axis_index("vocab")
    batch_index = lax.axis_index("batch")
    local_rows = embedding.shape[0]
    local_blocks = block_counts.shape[0]
    block_width = local_rows // local_blocks
    own_rows = local_rows // batch_count
    own_blocks = own_rows // block_width
    group_tokens = vocab_count * tok_dev
    order = centre_first(vocab_count)
    both = ("vocab", "batch")
    groups = [[v * batch_count + b for v in order] for b in range(batch_count)]

    copies = jnp.broadcast_to(hidden[None], (vocab_count, tok_dev, width))
    gathered = lax.all_to_all(copies, both, 0, 0, tiled=True, axis_index_groups=groups)
    gathered = gathered.reshape(group_tokens, width)
    pieces = [gathered]
    for step in range(1, batch_count):
        pairs = [(b, b ^ step) for b in range(batch_count)]
        pieces.append(lax.ppermute(gathered, "batch", pairs))
    everyone = jnp.concatenate(pieces, axis=0)

    sources = batch_index ^ jnp.arange(batch_count, dtype=jnp.int32)
    places = jnp.array(order, jnp.int32)
    token_ids = (
        (places[None, :, None] * batch_count + sources[:, None, None]) * tok_dev
        + jnp.arange(tok_dev, dtype=jnp.int32)[None, None, :]
    ).reshape(batch_count, group_tokens)
    target_table = targets.reshape(vocab_count, batch_count, tok_dev)
    target_table = jnp.stack([target_table[v] for v in order], axis=1)
    target_ids = jnp.stack(
        [
            lax.dynamic_index_in_dim(target_table, batch_index ^ step, 0, keepdims=False)
            for step in range(batch_count)
        ]
    ).reshape(batch_count, group_tokens)

    block_ids = vocab_index * local_blocks + jnp.arange(local_blocks, dtype=jnp.int32)
    sentence_lists = lang_blocks[sent_lang]
    member = jnp.any(sentence_lists[:, None, :] == block_ids[None, :, None], axis=2)
    sentence_ids = jnp.arange(sent_lang.shape[0], dtype=jnp.int32)
    sentence_hit = (token_ids // SEQ)[None] == sentence_ids[:, None, None]
    allowed = jnp.any(member[:, :, None, None] & sentence_hit[:, None], axis=0)
    log_sampling = jnp.log(block_counts.astype(jnp.float32))

    own_allowed = allowed[:, 0][:, None, :]
    logits = lax.dot_general(
        embedding, gathered, (((1,), (1,)), ((), ())), preferred_element_type=jnp.float32
    ).reshape(local_blocks, block_width, group_tokens) - log_sampling[:, None, None]
    word_ids = (vocab_index * local_rows + jnp.arange(local_rows, dtype=jnp.int32)).reshape(
        local_blocks, block_width
    )
    is_target = word_ids[:, :, None] == target_ids[0][None, None, :]
    local_peak = jnp.max(jnp.where(own_allowed, logits, masked_fill), axis=(0, 1))
    local_total = jnp.sum(
        jnp.where(own_allowed, jnp.exp(logits - local_peak[None, None, :]), 0.0), axis=(0, 1)
    )
    local_target = jnp.sum(jnp.where(is_target, logits, 0.0), axis=(0, 1))
    blank = jnp.zeros_like(local_peak)
    stats = jnp.stack([local_peak, local_total, local_target] + [blank] * 5)
    stats = jnp.broadcast_to(stats[None], (vocab_count * batch_count,) + stats.shape)
    stats = lax.all_to_all(stats, both, 0, 0, tiled=True)
    stats = stats.reshape(vocab_count, batch_count, 8, group_tokens)
    peak = jnp.max(stats[:, :, 0], axis=0)
    total = jnp.sum(stats[:, :, 1] * jnp.exp(stats[:, :, 0] - peak[None]), axis=0)
    log_total = peak + jnp.log(total)
    target_logit = jnp.sum(stats[:, :, 2], axis=0)
    every_loss = lax.dynamic_index_in_dim(log_total - target_logit, batch_index, 0, keepdims=False)
    my_place = jnp.sum(jnp.where(places == vocab_index, jnp.arange(vocab_count), 0))
    token_loss = lax.dynamic_slice_in_dim(every_loss, my_place * tok_dev, tok_dev, 0)
    ordered = jnp.stack(
        [
            lax.dynamic_index_in_dim(log_total, batch_index ^ step, 0, keepdims=False)
            for step in range(batch_count)
        ]
    ).reshape(-1)

    mine = lax.dynamic_slice_in_dim(embedding, batch_index * own_rows, own_rows, 0)
    my_blocks = batch_index * own_blocks
    my_sampling = lax.dynamic_slice_in_dim(log_sampling, my_blocks, own_blocks, 0)
    my_allowed = lax.dynamic_slice_in_dim(allowed, my_blocks, own_blocks, 0)
    my_allowed = my_allowed.reshape(own_blocks, 1, -1)
    my_words = lax.dynamic_slice_in_dim(word_ids, my_blocks, own_blocks, 0)
    my_logits = lax.dot_general(
        mine, everyone, (((1,), (1,)), ((), ())), preferred_element_type=jnp.float32
    ).reshape(own_blocks, block_width, -1) - my_sampling[:, None, None]
    weights = jnp.where(my_allowed, jnp.exp(my_logits - ordered[None, None, :]), 0.0)
    hits = my_words[:, :, None] == target_ids.reshape(-1)[None, None, :]
    grad_logits = (weights - hits.astype(jnp.float32)).astype(jnp.bfloat16)
    grad_embed = lax.dot_general(
        grad_logits.reshape(own_rows, -1),
        everyone,
        (((1,), (0,)), ((), ())),
        preferred_element_type=jnp.float32,
    ).astype(jnp.bfloat16)
    return (token_loss, grad_embed)


def solution(mesh):
    in_specs = (P(("vocab", "batch"), None), P("vocab", None), P("vocab"), P(), P(), P())
    out_specs = (P(("vocab", "batch")), P(("vocab", "batch"), None))

    def step(hidden, *rest):
        group_tokens = hidden.shape[0] * lax.axis_size("vocab")
        chosen = fused_body if (2 * group_tokens, lax.axis_size("batch")) == (LANES, 4) else body
        return chosen(hidden, *rest)

    return jax.shard_map(
        step, mesh=mesh, in_specs=in_specs, out_specs=out_specs, check_vma=False
    )
```
